256 devices in a mesh: ckpt: 8 (over z_hi, x), train: 32 (over y, z_lo, core).
Axes of the slice: x: 4, y: 4, z: 8 (z_hi: 2, z_lo: 4; z = z_hi * 4 + z_lo), core: 2. Of those that a mesh axis runs over, the one named last changes fastest.
Arguments:
- train_feat: bfloat16 [8, 65536, 1024], P('ckpt', 'train'), may hold values from -6 to 6
- test_feat: bfloat16 [8, 1024, 1024], P('ckpt', 'train'), may hold values from -0.375 to 0.375
- kernel_inv: bfloat16 [8, 1024, 1024], P('ckpt', 'train'), may hold values from -0.1875 to 0.1875
- bucket_weight: float32 [8, 16], P('ckpt'), may hold values from 0.2 to 2
- bucket: int32 [65536], P('train'), may hold values from 0 to 15
- test_order: int32 [1024], replicated, may hold values from 0 to 1023, each once
Outputs:
- scores: float32 [65536, 1024], P('train', 'ckpt')
The draws below stay inside these ranges and needn't reach their ends.
Inputs may be any that keep to these rules, and one draw needn't show every extreme that they name: `test_order`: each of 0 to 1023 once.
All inputs are finite; a program needn't handle non-finite values.
Results may differ from the reference program's by a relative error of at most 0.012.
Values may be sent and summed in bfloat16 or wider, within the bound.
A program may use at most 64 MiB of HBM per device.

```python
import math
import jax
import jax.numpy as jnp
from jax import lax

P_SIZE = 1024
NTEST = 1024
NB = 16
CK_DEV = 1
K = 8
NTRAIN = 65536
N_CKPT = 8


def with_ends(entries, key, low, high):
    extent = entries.shape
    index_at = [jax.random.randint(jax.random.fold_in(key, axis), (), 0, extent[axis]) for axis in range(len(extent))]
    entries = entries.at[tuple(index_at)].set(low)
    longest = extent.index(max(extent))
    index_at[longest] = (index_at[longest] + 1) % extent[longest]
    return entries.at[tuple(index_at)].set(high)


def levels(stream_key, shape, pieces, low, largest):
    gain, own = 1.0, jax.random.fold_in(stream_key, 6)
    for dim, parts in pieces:
        steps = jnp.exp(jax.random.uniform(jax.random.fold_in(own, dim), (parts,), jnp.float32, low / len(pieces), largest / len(pieces)))
        gain = gain * jnp.repeat(steps, shape[dim] // parts).reshape([-1 if axis == dim else 1 for axis in range(len(shape))])
    return gain


def noise(own_key, shape, deviation, reach, shards=(), dtype=jnp.bfloat16):
    gain = levels(own_key, shape, shards, -0.22, 0.18) if shards else 1.0
    array = jax.random.normal(own_key, shape, jnp.float32) * deviation * gain
    return jnp.minimum(jnp.maximum(array, -reach), reach).astype(dtype)


def setup_inputs(seed: int = 0) -> dict:
    streams_of = jax.random.split(jax.random.key(seed), 7)
    return {
        "train_feat": noise(streams_of[0], (K, NTRAIN, P_SIZE), 1.0, 6.0, ((0, 8), (1, 32))),
        "test_feat": noise(streams_of[1], (K, NTEST, P_SIZE), 0.0625, 0.375, ((0, 8), (1, 32))),
        "kernel_inv": noise(streams_of[2], (K, P_SIZE, P_SIZE), P_SIZE ** -0.5, 0.1875, ((0, 8), (1, 32))),
        "bucket_weight": jnp.clip(jnp.exp(math.log(2.0) - 2.3025851 * jax.random.uniform(streams_of[3], (K, NB), jnp.float32) ** levels(streams_of[3], (K, NB), ((0, 8),), -0.2, 0.2)), 0.2, 2.0),
        "bucket": with_ends(jax.random.randint(streams_of[4], (NTRAIN,), 0, NB), jax.random.fold_in(streams_of[4], 1), 0, NB - 1).astype(jnp.int32),
        "test_order": jax.random.permutation(streams_of[5], NTEST).astype(jnp.int32),
    }


def reference(train_feat, test_feat, kernel_inv, bucket_weight, bucket, test_order):
    acc = jnp.zeros((NTRAIN, NTEST), jnp.float32)
    for group_idx in range(N_CKPT):
        partial_sum = jnp.zeros((NTRAIN, NTEST), jnp.float32)
        for inner in range(CK_DEV):
            k = group_idx * CK_DEV + inner
            transformed = jnp.einsum("jb,ab->ja", test_feat[k], kernel_inv[k], preferred_element_type=jnp.float32).astype(jnp.bfloat16)
            ordered = jnp.zeros_like(transformed).at[test_order].set(transformed)
            weight = bucket_weight[k][bucket]
            partial_sum = partial_sum + weight[:, None] * jnp.dot(train_feat[k], ordered.T, preferred_element_type=jnp.float32)
        rounded = lax.optimization_barrier(partial_sum.astype(jnp.bfloat16))
        acc = acc + rounded.astype(jnp.float32)
    return acc / K
```

```python
import functools

import jax
import jax.numpy as jnp
from jax import lax
from jax.experimental import pallas as pl
from jax.experimental.pallas import tpu as pltpu
from jax.sharding import PartitionSpec as P

MESH = pl.DeviceIdType.MESH
F32 = jnp.float32
BF16 = jnp.bfloat16
ROWS = 256
NT = (((1,), (1,)), ((), ()))
TN = (((0,), (0,)), ((), ()))


def kernel(
    train_hbm, test_hbm, kinv_hbm, bw_ref, bucket_ref, order_ref, out_ref,
    train, gb, tp, ob, wcol, s2, sp, sm, far_l, far_r, got_l, got_r, own, zs, zr,
    load_sem, g_send, g_recv, sib_send, sib_recv, s2_send, sp_send, sm_send,
    far_l_recv, far_r_recv, got_l_recv, got_r_recv, z_send, z_recv,
):
    ck = lax.axis_index("ckpt")
    tr = lax.axis_index("train")
    zh, x = ck // 4, ck % 4
    y, z, c = tr // 8, (tr // 2) % 4, tr % 2

    def at_train(yy, zz, cc):
        return {"ckpt": ck, "train": (yy * 4 + zz) * 2 + cc}

    def at_ckpt(zz, xx):
        return {"ckpt": zz * 4 + xx, "train": tr}

    fold = z // 2
    w = z + fold * (3 - 2 * z)

    def zplace(s):
        if s == 0:
            return z
        v = s - 1 + (s - 1 - w + 4) // 4
        return v + fold * (3 - 2 * v)

    y_up, y_dn, y_far = (y + 1) % 4, (y + 3) % 4, (y + 2) % 4
    up, dn = at_train(y_up, z, c), at_train(y_dn, z, c)
    sib = at_train(y, z, 1 - c)
    right, left = at_ckpt(zh, (x + 1) % 4), at_ckpt(zh, (x + 3) % 4)
    across = at_ckpt(1 - zh, x)

    loads = [
        pltpu.make_async_copy(test_hbm, gb.at[0, tr], load_sem.at[0]),
        pltpu.make_async_copy(kinv_hbm, gb.at[1, tr], load_sem.at[1]),
        pltpu.make_async_copy(train_hbm, train, load_sem.at[2]),
    ]
    for cp in loads:
        cp.start()

    barrier = pltpu.get_barrier_semaphore()
    partners = [up, dn, sib, right, left, across]
    partners += [at_train(y, zplace(s), c) for s in (1, 2, 3)]
    for d in partners:
        pl.semaphore_signal(barrier, inc=1, device_id=d, device_id_type=MESH)
    pl.semaphore_wait(barrier, len(partners))
    loads[0].wait()
    loads[1].wait()

    started = []
    counts = [0, 0]

    def g_copy(m, yy, zz, send, dev):
        chunk = (yy * 4 + zz) * 2 + c
        return pltpu.make_async_remote_copy(
            src_ref=gb.at[m, chunk], dst_ref=gb.at[m, chunk], send_sem=send,
            recv_sem=g_recv.at[m, yy, zz], device_id=dev, device_id_type=MESH,
        )

    def g_start(m, yy, zz, dev):
        cp = g_copy(m, yy, zz, g_send.at[m, counts[m]], dev)
        counts[m] += 1
        cp.start()
        started.append(cp)

    def g_wait(m, yy, zz):
        g_copy(m, yy, zz, g_send.at[m, 0], up).wait_recv()

    def sib_copy(m, yy, zz, cc):
        chunk = (yy * 4 + zz) * 2 + cc
        return pltpu.make_async_remote_copy(
            src_ref=gb.at[m, chunk], dst_ref=gb.at[m, chunk], send_sem=sib_send.at[m, yy, zz],
            recv_sem=sib_recv.at[m, yy, zz], device_id=sib, device_id_type=MESH,
        )

    def to_sib(m, yy, zz):
        cp = sib_copy(m, yy, zz, c)
        cp.start()
        started.append(cp)

    def begin(m):
        g_start(m, y, z, up)
        g_start(m, y, z, dn)
        for s in (1, 2, 3):
            g_start(m, y, z, at_train(y, zplace(s), c))
        to_sib(m, y, z)

    def from_line(m, s):
        zz = zplace(s)
        g_wait(m, y, zz)
        g_start(m, y, zz, up)
        g_start(m, y, zz, dn)
        to_sib(m, y, zz)

    def from_ring(m, s):
        zz = zplace(s)
        g_wait(m, y_dn, zz)
        if s % 2 == 0:
            g_start(m, y_dn, zz, up)
        to_sib(m, y_dn, zz)
        g_wait(m, y_up, zz)
        if s % 2 == 1:
            g_start(m, y_up, zz, dn)
        to_sib(m, y_up, zz)

    def from_far(m, s):
        zz = zplace(s)
        g_wait(m, y_far, zz)
        to_sib(m, y_far, zz)

    def from_sib(m):
        def step(i, carry):
            sib_copy(m, i // 4, i % 4, 1 - c).wait_recv()
            return carry
        lax.fori_loop(0, 16, step, 0)

    def blocks(h, p):
        side = zh if h == 1 else 1 - zh
        first, second = ((x + 2) % 4, x) if p == 0 else ((x + 1) % 4, (x + 3) % 4)
        return (side * 4 + first) * 128, (side * 4 + second) * 128

    def permute(h, p):
        a, b = blocks(h, p)
        order = order_ref[...]
        j = lax.broadcasted_iota(jnp.int32, (128, 1), 0)
        pick = jnp.concatenate(
            [(order == j + a).astype(F32).astype(BF16), (order == j + b).astype(F32).astype(BF16)], axis=0
        )

        def step(i, carry):
            cols = pl.ds(pl.multiple_of(i * 256, 256), 256)
            rows = gb[0, :, :, cols].reshape(1024, 256)
            tp[2 * h + p, :, cols] = jnp.dot(pick, rows, preferred_element_type=F32).astype(BF16)
            return carry
        lax.fori_loop(0, 4, step, 0)

    def transform(h, p):
        def step(i, carry):
            inv = gb[1, pl.ds(i * 8, 8)].reshape(256, 1024)
            cols = pl.ds(pl.multiple_of(i * 256, 256), 256)
            ob[2 * h + p, :, cols] = lax.dot_general(
                tp[2 * h + p], inv, NT, preferred_element_type=F32
            ).astype(BF16)
            return carry
        lax.fori_loop(0, 4, step, 0)

    begin(0)
    begin(1)

    eye = lax.broadcasted_iota(jnp.int32, (16, 16), 0) == lax.broadcasted_iota(jnp.int32, (16, 16), 1)
    col = jnp.sum(jnp.where(eye, jnp.broadcast_to(bw_ref[...], (16, 16)), 0.0), axis=1, keepdims=True)
    col = jnp.broadcast_to(col, (16, 128))
    hi = col.astype(BF16)
    rest = col - hi.astype(F32)
    mid = rest.astype(BF16)
    low = (rest - mid.astype(F32)).astype(BF16)

    def weigh(i, carry):
        rows = pl.ds(pl.multiple_of(i * ROWS, ROWS), ROWS)
        b = bucket_ref[:, rows]
        hot = (lax.broadcasted_iota(jnp.int32, (16, 1), 0) == b).astype(F32).astype(BF16)
        acc = lax.dot_general(hot, hi, TN, preferred_element_type=F32)
        acc += lax.dot_general(hot, mid, TN, preferred_element_type=F32)
        acc += lax.dot_general(hot, low, TN, preferred_element_type=F32)
        wcol[i] = acc
        return carry
    lax.fori_loop(0, 8, weigh, 0)

    from_line(0, 1)
    from_ring(0, 0)
    from_line(0, 2)
    from_ring(0, 1)
    from_ring(1, 0)
    from_line(0, 3)
    from_ring(0, 2)
    from_line(1, 1)
    from_ring(0, 3)
    from_line(1, 2)
    from_ring(1, 1)
    for s in range(4):
        from_far(0, s)
    from_line(1, 3)
    from_sib(0)
    permute(0, 0)
    from_ring(1, 2)
    permute(0, 1)
    from_ring(1, 3)
    permute(1, 0)
    from_far(1, 0)
    from_far(1, 1)
    from_far(1, 2)
    permute(1, 1)
    from_far(1, 3)
    loads[2].wait()
    from_sib(1)

    def tile(r, k):
        rows = pl.ds(pl.multiple_of(r * ROWS, ROWS), ROWS)
        t = lax.dot_general(train[rows, :], ob[k], NT, preferred_element_type=F32)
        return t[:, :128] * wcol[r], t[:, 128:] * wcol[r]

    def far_copy(h, i, r, to_right):
        return pltpu.make_async_remote_copy(
            src_ref=s2.at[h, r], dst_ref=(far_l if to_right else far_r).at[h, i], send_sem=s2_send.at[h, r],
            recv_sem=(far_l_recv if to_right else far_r_recv).at[h, i],
            device_id=right if to_right else left, device_id_type=MESH,
        )

    def right_copy(h, r):
        return pltpu.make_async_remote_copy(
            src_ref=sp.at[h, r], dst_ref=got_l.at[h, r], send_sem=sp_send.at[h, r],
            recv_sem=got_l_recv.at[h, r], device_id=right, device_id_type=MESH,
        )

    def left_copy(h, r):
        return pltpu.make_async_remote_copy(
            src_ref=sm.at[h, r], dst_ref=got_r.at[h, r], send_sem=sm_send.at[h, r],
            recv_sem=got_r_recv.at[h, r], device_id=left, device_id_type=MESH,
        )

    def z_copy(r):
        return pltpu.make_async_remote_copy(
            src_ref=zs.at[r], dst_ref=zr.at[r], send_sem=z_send.at[r],
            recv_sem=z_recv.at[r], device_id=across, device_id_type=MESH,
        )

    def far_blocks(h):
        def step(i, carry):
            for half in (0, 1):
                r = i + 4 * half
                a, b = tile(r, 2 * h)
                s2[h, r] = a.astype(BF16)
                own[h, r] = b
                far_copy(h, i, r, half == 0).start()
            return carry
        lax.fori_loop(0, 4, step, 0)

    def near_blocks(h):
        def step(i, carry):
            p, m = tile(i, 2 * h + 1)
            sm[h, i] = m.astype(BF16)
            left_copy(h, i).start()
            far_copy(h, i, i, True).wait_recv()
            sp[h, i] = (p + far_l[h, i].astype(F32)).astype(BF16)
            right_copy(h, i).start()
            r = i + 4
            p, m = tile(r, 2 * h + 1)
            sp[h, r] = p.astype(BF16)
            right_copy(h, r).start()
            far_copy(h, i, r, False).wait_recv()
            sm[h, r] = (m + far_r[h, i].astype(F32)).astype(BF16)
            left_copy(h, r).start()
            return carry
        lax.fori_loop(0, 4, step, 0)

    def add_up(h):
        def step(i, carry):
            for half in (0, 1):
                r = i + 4 * half
                right_copy(h, r).wait_recv()
                left_copy(h, r).wait_recv()
                v = own[h, r] + got_l[h, r].astype(F32) + got_r[h, r].astype(F32)
                if h == 0:
                    zs[r] = v.astype(BF16)
                    z_copy(r).start()
                else:
                    own[h, r] = v
            return carry
        lax.fori_loop(0, 4, step, 0)

    transform(0, 0)
    far_blocks(0)
    transform(0, 1)
    near_blocks(0)
    transform(1, 0)
    far_blocks(1)
    transform(1, 1)
    add_up(0)
    near_blocks(1)
    add_up(1)

    def finish(i, carry):
        for half in (0, 1):
            r = i + 4 * half
            z_copy(r).wait_recv()
            rows = pl.ds(pl.multiple_of(r * ROWS, ROWS), ROWS)
            out_ref[rows, :] = (own[1, r] + zr[r].astype(F32)) * 0.125
        return carry
    lax.fori_loop(0, 4, finish, 0)

    for cp in started:
        cp.wait_send()

    def drain(r, carry):
        for h in (0, 1):
            far_copy(h, 0, r, True).wait_send()
            right_copy(h, r).wait_send()
            left_copy(h, r).wait_send()
        z_copy(r).wait_send()
        return carry
    lax.fori_loop(0, 8, drain, 0)


def shards(train_feat, test_feat, kernel_inv, bucket_weight, bucket, test_order):
    anywhere = pl.BlockSpec(memory_space=pl.ANY)
    vmem = pl.BlockSpec(memory_space=pltpu.VMEM)
    dma = pltpu.SemaphoreType.DMA
    return pl.pallas_call(
        kernel,
        out_shape=jax.ShapeDtypeStruct((2048, 128), F32),
        in_specs=[anywhere, anywhere, anywhere, vmem, vmem, vmem],
        out_specs=vmem,
        scratch_shapes=[
            pltpu.VMEM((2048, 1024), BF16),
            pltpu.VMEM((2, 32, 32, 1024), BF16),
            pltpu.VMEM((4, 256, 1024), BF16),
            pltpu.VMEM((4, 256, 1024), BF16),
            pltpu.VMEM((8, ROWS, 128), F32),
            pltpu.VMEM((2, 8, ROWS, 128), BF16),
            pltpu.VMEM((2, 8, ROWS, 128), BF16),
            pltpu.VMEM((2, 8, ROWS, 128), BF16),
            pltpu.VMEM((2, 4, ROWS, 128), BF16),
            pltpu.VMEM((2, 4, ROWS, 128), BF16),
            pltpu.VMEM((2, 8, ROWS, 128), BF16),
            pltpu.VMEM((2, 8, ROWS, 128), BF16),
            pltpu.VMEM((2, 8, ROWS, 128), F32),
            pltpu.VMEM((8, ROWS, 128), BF16),
            pltpu.VMEM((8, ROWS, 128), BF16),
            dma((3,)),
            dma((2, 16)),
            dma((2, 4, 4)),
            dma((2, 4, 4)),
            dma((2, 4, 4)),
            dma((2, 8)),
            dma((2, 8)),
            dma((2, 8)),
            dma((2, 4)),
            dma((2, 4)),
            dma((2, 8)),
            dma((2, 8)),
            dma((8,)),
            dma((8,)),
        ],
        compiler_params=pltpu.CompilerParams(
            collective_id=0, has_side_effects=True, vmem_limit_bytes=60 * 1024 * 1024
        ),
        name="scores",
    )(
        train_feat[0], test_feat[0], kernel_inv[0], bucket_weight,
        bucket.reshape(1, 2048), test_order.reshape(1, 1024),
    )


def solution(mesh):
    return jax.shard_map(
        shards, mesh=mesh,
        in_specs=(P("ckpt", "train", None), P("ckpt", "train", None), P("ckpt", "train", None),
                  P("ckpt", None), P("train"), P(None)),
        out_specs=P("train", "ckpt"), check_vma=False,
    )
```

```python
import functools

import jax
import jax.numpy as jnp
from jax import lax
from jax.experimental import pallas as pl
from jax.experimental.pallas import tpu as pltpu
from jax.sharding import PartitionSpec as P

MESH = pl.DeviceIdType.MESH
F32 = jnp.float32
BF16 = jnp.bfloat16
ROWS = 256
NT = (((1,), (1,)), ((), ()))
TN = (((0,), (0,)), ((), ()))


def kernel(
    train_hbm, test_hbm, kinv_hbm, bw_ref, bucket_ref, order_ref, out_ref,
    train, tb, kb, gb, ob, wcol, s2, sp, sm, far_l, far_r, got_l, got_r, own, zs, zr,
    load_sem, t_send, t_recv, k_send, k_recv, k_sib, b_send, b_recv, b_sib, s2_send, sp_send, sm_send,
    far_l_recv, far_r_recv, got_l_recv, got_r_recv, z_send, z_recv,
):
    ck = lax.axis_index("ckpt")
    tr = lax.axis_index("train")
    zh, x = ck // 4, ck % 4
    y, z, c = tr // 8, (tr // 2) % 4, tr % 2

    def at_train(yy, zz, cc):
        return {"ckpt": ck, "train": (yy * 4 + zz) * 2 + cc}

    def at_ckpt(zz, xx):
        return {"ckpt": zz * 4 + xx, "train": tr}

    fold = z // 2
    w = z + fold * (3 - 2 * z)

    def zplace(s):
        if s == 0:
            return z
        v = s - 1 + (s - 1 - w + 4) // 4
        return v + fold * (3 - 2 * v)

    y_up, y_dn, y_far = (y + 1) % 4, (y + 3) % 4, (y + 2) % 4
    up, dn = at_train(y_up, z, c), at_train(y_dn, z, c)
    sib = at_train(y, z, 1 - c)
    right, left = at_ckpt(zh, (x + 1) % 4), at_ckpt(zh, (x + 3) % 4)
    across = at_ckpt(1 - zh, x)

    loads = [
        pltpu.make_async_copy(test_hbm, tb.at[y], load_sem.at[0]),
        pltpu.make_async_copy(kinv_hbm, kb.at[z, c], load_sem.at[1]),
        pltpu.make_async_copy(train_hbm, train, load_sem.at[2]),
    ]
    for cp in loads:
        cp.start()

    barrier = pltpu.get_barrier_semaphore()
    partners = [up, dn, at_train(y_far, z, c), sib, right, left, across]
    partners += [at_train(y, zplace(s), c) for s in (1, 2, 3)]
    for d in partners:
        pl.semaphore_signal(barrier, inc=1, device_id=d, device_id_type=MESH)
    pl.semaphore_wait(barrier, len(partners))

    started = []

    def send(ref, send_sem, recv_sem, dev):
        cp = pltpu.make_async_remote_copy(
            src_ref=ref, dst_ref=ref, send_sem=send_sem, recv_sem=recv_sem, device_id=dev, device_id_type=MESH,
        )
        cp.start()
        started.append(cp)

    def arrived(ref, recv_sem):
        pltpu.make_async_remote_copy(
            src_ref=ref, dst_ref=ref, send_sem=b_send.at[0], recv_sem=recv_sem, device_id=sib, device_id_type=MESH,
        ).wait_recv()

    ring = [at_train(y_far, z, c), up, dn]

    loads[1].wait()
    for s in (1, 2, 3):
        send(kb.at[z, c], k_send.at[s], k_recv.at[z], at_train(y, zplace(s), c))
    send(kb.at[z, c], k_send.at[0], k_sib.at[z], sib)
    loads[0].wait()
    for i, d in enumerate(ring):
        send(tb.at[y], t_send.at[i], t_recv.at[y], d)

    eye = lax.broadcasted_iota(jnp.int32, (16, 16), 0) == lax.broadcasted_iota(jnp.int32, (16, 16), 1)
    col = jnp.sum(jnp.where(eye, jnp.broadcast_to(bw_ref[...], (16, 16)), 0.0), axis=1, keepdims=True)
    col = jnp.broadcast_to(col, (16, 128))
    hi = col.astype(BF16)
    rest = col - hi.astype(F32)
    mid = rest.astype(BF16)
    low = (rest - mid.astype(F32)).astype(BF16)

    def weigh(i, carry):
        rows = pl.ds(pl.multiple_of(i * ROWS, ROWS), ROWS)
        b = bucket_ref[:, rows]
        hot = (lax.broadcasted_iota(jnp.int32, (16, 1), 0) == b).astype(F32).astype(BF16)
        acc = lax.dot_general(hot, hi, TN, preferred_element_type=F32)
        acc += lax.dot_general(hot, mid, TN, preferred_element_type=F32)
        acc += lax.dot_general(hot, low, TN, preferred_element_type=F32)
        wcol[i] = acc
        return carry
    lax.fori_loop(0, 8, weigh, 0)

    for s in (1, 2, 3):
        zz = zplace(s)
        arrived(kb.at[zz, c], k_recv.at[zz])
        send(kb.at[zz, c], k_send.at[3 + s], k_sib.at[zz], sib)
    for yy in (y_up, y_dn, y_far):
        arrived(tb.at[yy], t_recv.at[yy])
    for s in range(4):
        zz = zplace(s)
        arrived(kb.at[zz, 1 - c], k_sib.at[zz])

    block = lax.dot_general(
        tb[...].reshape(128, 1024), kb[...].reshape(256, 1024), NT, preferred_element_type=F32
    ).astype(BF16)
    gb[y, :, z, c] = block.reshape(4, 32, 256)

    def part(yy, zz, cc):
        return gb.at[yy, :, zz, cc]

    for s in (1, 2, 3):
        send(part(y, z, c), b_send.at[s], b_recv.at[y, z], at_train(y, zplace(s), c))
    for i, d in enumerate(ring):
        send(part(y, z, c), b_send.at[4 + i], b_recv.at[y, z], d)
    send(part(y, z, c), b_send.at[0], b_sib.at[y, z], sib)
    for s in (1, 2, 3):
        zz = zplace(s)
        arrived(part(y, zz, c), b_recv.at[y, zz])
        for i, d in enumerate(ring):
            send(part(y, zz, c), b_send.at[4 + 3 * s + i], b_recv.at[y, zz], d)
        send(part(y, zz, c), b_send.at[15 + s], b_sib.at[y, zz], sib)
    for s in range(4):
        zz = zplace(s)
        for i, yy in enumerate((y_up, y_dn, y_far)):
            arrived(part(yy, zz, c), b_recv.at[yy, zz])
            send(part(yy, zz, c), b_send.at[19 + 3 * s + i], b_sib.at[yy, zz], sib)

    def blocks(h, p):
        side = zh if h == 1 else 1 - zh
        first, second = ((x + 2) % 4, x) if p == 0 else ((x + 1) % 4, (x + 3) % 4)
        return (side * 4 + first) * 128, (side * 4 + second) * 128

    def permute(h, p, yy):
        a, b = blocks(h, p)
        order = order_ref[...]
        j = lax.broadcasted_iota(jnp.int32, (128, 1), 0)
        pick = jnp.concatenate(
            [(order == j + a).astype(F32).astype(BF16), (order == j + b).astype(F32).astype(BF16)], axis=0
        )
        rows = gb[yy].reshape(1024, 256)
        cols = pl.ds(pl.multiple_of(yy * 256, 256), 256)
        ob[2 * h + p, :, cols] = jnp.dot(pick, rows, preferred_element_type=F32).astype(BF16)

    def permute_all(h, p):
        def step(yy, carry):
            permute(h, p, yy)
            return carry
        lax.fori_loop(0, 4, step, 0)

    loads[2].wait()
    for yy in (y, y_up, y_dn, y_far):
        for s in range(4):
            zz = zplace(s)
            arrived(part(yy, zz, 1 - c), b_sib.at[yy, zz])
        permute(0, 0, yy)

    def tile(r, k):
        rows = pl.ds(pl.multiple_of(r * ROWS, ROWS), ROWS)
        t = lax.dot_general(train[rows, :], ob[k], NT, preferred_element_type=F32)
        return t[:, :128] * wcol[r], t[:, 128:] * wcol[r]

    def far_copy(h, i, r, to_right):
        return pltpu.make_async_remote_copy(
            src_ref=s2.at[h, r], dst_ref=(far_l if to_right else far_r).at[h, i], send_sem=s2_send.at[h, r],
            recv_sem=(far_l_recv if to_right else far_r_recv).at[h, i],
            device_id=right if to_right else left, device_id_type=MESH,
        )

    def right_copy(h, r):
        return pltpu.make_async_remote_copy(
            src_ref=sp.at[h, r], dst_ref=got_l.at[h, r], send_sem=sp_send.at[h, r],
            recv_sem=got_l_recv.at[h, r], device_id=right, device_id_type=MESH,
        )

    def left_copy(h, r):
        return pltpu.make_async_remote_copy(
            src_ref=sm.at[h, r], dst_ref=got_r.at[h, r], send_sem=sm_send.at[h, r],
            recv_sem=got_r_recv.at[h, r], device_id=left, device_id_type=MESH,
        )

    def z_copy(r):
        return pltpu.make_async_remote_copy(
            src_ref=zs.at[r], dst_ref=zr.at[r], send_sem=z_send.at[r],
            recv_sem=z_recv.at[r], device_id=across, device_id_type=MESH,
        )

    def far_blocks(h):
        def step(i, carry):
            for half in (0, 1):
                r = i + 4 * half
                a, b = tile(r, 2 * h)
                s2[h, r] = a.astype(BF16)
                own[h, r] = b
                far_copy(h, i, r, half == 0).start()
            return carry
        lax.fori_loop(0, 4, step, 0)

    def near_blocks(h):
        def step(i, carry):
            p, m = tile(i, 2 * h + 1)
            sm[h, i] = m.astype(BF16)
            left_copy(h, i).start()
            far_copy(h, i, i, True).wait_recv()
            sp[h, i] = (p + far_l[h, i].astype(F32)).astype(BF16)
            right_copy(h, i).start()
            r = i + 4
            p, m = tile(r, 2 * h + 1)
            sp[h, r] = p.astype(BF16)
            right_copy(h, r).start()
            far_copy(h, i, r, False).wait_recv()
            sm[h, r] = (m + far_r[h, i].astype(F32)).astype(BF16)
            left_copy(h, r).start()
            return carry
        lax.fori_loop(0, 4, step, 0)

    def add_up(h):
        def step(i, carry):
            for half in (0, 1):
                r = i + 4 * half
                right_copy(h, r).wait_recv()
                left_copy(h, r).wait_recv()
                v = own[h, r] + got_l[h, r].astype(F32) + got_r[h, r].astype(F32)
                if h == 0:
                    zs[r] = v.astype(BF16)
                    z_copy(r).start()
                else:
                    z_copy(r).wait_recv()
                    rows = pl.ds(pl.multiple_of(r * ROWS, ROWS), ROWS)
                    out_ref[rows, :] = (v + zr[r].astype(F32)) * 0.125
            return carry
        lax.fori_loop(0, 4, step, 0)

    far_blocks(0)
    permute_all(0, 1)
    near_blocks(0)
    permute_all(1, 0)
    far_blocks(1)
    permute_all(1, 1)
    add_up(0)
    near_blocks(1)
    add_up(1)

    for cp in started:
        cp.wait_send()

    def drain(r, carry):
        for h in (0, 1):
            far_copy(h, 0, r, True).wait_send()
            right_copy(h, r).wait_send()
            left_copy(h, r).wait_send()
        z_copy(r).wait_send()
        return carry
    lax.fori_loop(0, 8, drain, 0)


def shards(train_feat, test_feat, kernel_inv, bucket_weight, bucket, test_order):
    anywhere = pl.BlockSpec(memory_space=pl.ANY)
    vmem = pl.BlockSpec(memory_space=pltpu.VMEM)
    dma = pltpu.SemaphoreType.DMA
    return pl.pallas_call(
        kernel,
        out_shape=jax.ShapeDtypeStruct((2048, 128), F32),
        in_specs=[anywhere, anywhere, anywhere, vmem, vmem, vmem],
        out_specs=vmem,
        scratch_shapes=[
            pltpu.VMEM((2048, 1024), BF16),
            pltpu.VMEM((4, 32, 1024), BF16),
            pltpu.VMEM((4, 2, 32, 1024), BF16),
            pltpu.VMEM((4, 4, 4, 2, 32, 256), BF16),
            pltpu.VMEM((4, 256, 1024), BF16),
            pltpu.VMEM((8, ROWS, 128), F32),
            pltpu.VMEM((2, 8, ROWS, 128), BF16),
            pltpu.VMEM((2, 8, ROWS, 128), BF16),
            pltpu.VMEM((2, 8, ROWS, 128), BF16),
            pltpu.VMEM((2, 4, ROWS, 128), BF16),
            pltpu.VMEM((2, 4, ROWS, 128), BF16),
            pltpu.VMEM((2, 8, ROWS, 128), BF16),
            pltpu.VMEM((2, 8, ROWS, 128), BF16),
            pltpu.VMEM((2, 8, ROWS, 128), F32),
            pltpu.VMEM((8, ROWS, 128), BF16),
            pltpu.VMEM((8, ROWS, 128), BF16),
            dma((3,)),
            dma((3,)),
            dma((4,)),
            dma((7,)),
            dma((4,)),
            dma((4,)),
            dma((31,)),
            dma((4, 4)),
            dma((4, 4)),
            dma((2, 8)),
            dma((2, 8)),
            dma((2, 8)),
            dma((2, 4)),
            dma((2, 4)),
            dma((2, 8)),
            dma((2, 8)),
            dma((8,)),
            dma((8,)),
        ],
        compiler_params=pltpu.CompilerParams(
            collective_id=0, has_side_effects=True, vmem_limit_bytes=60 * 1024 * 1024
        ),
        name="scores",
    )(
        train_feat[0], test_feat[0], kernel_inv[0], bucket_weight,
        bucket.reshape(1, 2048), test_order.reshape(1, 1024),
    )


def solution(mesh):
    return jax.shard_map(
        shards, mesh=mesh,
        in_specs=(P("ckpt", "train", None), P("ckpt", "train", None), P("ckpt", "train", None),
                  P("ckpt", None), P("train"), P(None)),
        out_specs=P("train", "ckpt"), check_vma=False,
    )
```

```python
import functools

import jax
import jax.numpy as jnp
from jax import lax
from jax.experimental import pallas as pl
from jax.experimental.pallas import tpu as pltpu
from jax.sharding import PartitionSpec as P

MESH = pl.DeviceIdType.MESH
F32 = jnp.float32
BF16 = jnp.bfloat16
ROWS = 256
NT = (((1,), (1,)), ((), ()))
TN = (((0,), (0,)), ((), ()))


def kernel(
    train_hbm, test_hbm, kinv_hbm, bw_hbm, bucket_hbm, order_hbm, out_ref,
    bw_ref, bucket_ref, order_ref, train, tb, kb, gb, ob, wcol, s2, sp, sm, far_l, far_r, got_l, got_r, own, zs, zr, zf,
    ready, out_sem, load_sem, t_send, t_recv, k_send, k_recv, k_sib, b_send, b_recv, b_sib, s2_send, sp_send, sm_send,
    far_l_recv, far_r_recv, got_l_recv, got_r_recv, z_send, z_recv, zf_recv,
):
    ck = lax.axis_index("ckpt")
    tr = lax.axis_index("train")
    zh, x = ck // 4, ck % 4
    y, z, c = tr // 8, (tr // 2) % 4, tr % 2

    def at_train(yy, zz, cc):
        return {"ckpt": ck, "train": (yy * 4 + zz) * 2 + cc}

    def at_ckpt(zz, xx):
        return {"ckpt": zz * 4 + xx, "train": tr}

    fold = z // 2
    w = z + fold * (3 - 2 * z)

    def zplace(s):
        if s == 0:
            return z
        v = s - 1 + (s - 1 - w + 4) // 4
        return v + fold * (3 - 2 * v)

    y_up, y_dn, y_far = (y + 1) % 4, (y + 3) % 4, (y + 2) % 4
    up, dn = at_train(y_up, z, c), at_train(y_dn, z, c)
    sib = at_train(y, z, 1 - c)
    right, left = at_ckpt(zh, (x + 1) % 4), at_ckpt(zh, (x + 3) % 4)
    across = at_ckpt(1 - zh, x)

    barrier = pltpu.get_barrier_semaphore()
    partners = [at_train(y, zplace(s), c) for s in (1, 2, 3)]
    partners += [up, dn, at_train(y_far, z, c), right, left, sib]
    for d in partners:
        pl.semaphore_signal(barrier, inc=1, device_id=d, device_id_type=MESH)

    @pl.when(zh == 0)
    def _():
        pl.semaphore_signal(barrier, inc=1, device_id=across, device_id_type=MESH)

    loads = [
        pltpu.make_async_copy(src, dst, load_sem.at[i])
        for i, (src, dst) in enumerate((
            (kinv_hbm, kb.at[z, c]), (test_hbm, tb.at[y]), (bw_hbm, bw_ref),
            (bucket_hbm, bucket_ref), (order_hbm, order_ref), (train_hbm, train),
        ))
    ]
    for cp in loads:
        cp.start()
    pl.semaphore_wait(barrier, len(partners) + zh)

    @pl.when(zh == 1)
    def _():
        pl.semaphore_signal(ready, inc=1, device_id=across, device_id_type=MESH)

    started = []

    def send(ref, send_sem, recv_sem, dev):
        cp = pltpu.make_async_remote_copy(
            src_ref=ref, dst_ref=ref, send_sem=send_sem, recv_sem=recv_sem, device_id=dev, device_id_type=MESH,
        )
        cp.start()
        started.append(cp)

    def arrived(ref, recv_sem):
        pltpu.make_async_remote_copy(
            src_ref=ref, dst_ref=ref, send_sem=b_send.at[0], recv_sem=recv_sem, device_id=sib, device_id_type=MESH,
        ).wait_recv()

    ring = [at_train(y_far, z, c), up, dn]

    loads[0].wait()
    for s in (1, 2, 3):
        send(kb.at[z, c], k_send.at[s], k_recv.at[z], at_train(y, zplace(s), c))
    send(kb.at[z, c], k_send.at[0], k_sib.at[z], sib)
    loads[1].wait()
    for i, d in enumerate(ring):
        send(tb.at[y], t_send.at[i], t_recv.at[y], d)

    for i in (2, 3, 4):
        loads[i].wait()

    eye = lax.broadcasted_iota(jnp.int32, (16, 16), 0) == lax.broadcasted_iota(jnp.int32, (16, 16), 1)
    col = jnp.sum(jnp.where(eye, jnp.broadcast_to(bw_ref[...], (16, 16)), 0.0), axis=1, keepdims=True)
    col = jnp.broadcast_to(col, (16, 128))
    hi = col.astype(BF16)
    rest = col - hi.astype(F32)
    mid = rest.astype(BF16)
    low = (rest - mid.astype(F32)).astype(BF16)

    def weigh(i, carry):
        rows = pl.ds(pl.multiple_of(i * ROWS, ROWS), ROWS)
        b = bucket_ref[:, rows]
        hot = (lax.broadcasted_iota(jnp.int32, (16, 1), 0) == b).astype(F32).astype(BF16)
        acc = lax.dot_general(hot, hi, TN, preferred_element_type=F32)
        acc += lax.dot_general(hot, mid, TN, preferred_element_type=F32)
        acc += lax.dot_general(hot, low, TN, preferred_element_type=F32)
        wcol[i] = acc
        return carry
    lax.fori_loop(0, 8, weigh, 0)

    for s in (1, 2, 3):
        zz = zplace(s)
        arrived(kb.at[zz, c], k_recv.at[zz])
        send(kb.at[zz, c], k_send.at[3 + s], k_sib.at[zz], sib)
    for yy in (y_up, y_dn, y_far):
        arrived(tb.at[yy], t_recv.at[yy])
    for s in range(4):
        zz = zplace(s)
        arrived(kb.at[zz, 1 - c], k_sib.at[zz])

    block = lax.dot_general(
        tb[...].reshape(128, 1024), kb[...].reshape(256, 1024), NT, preferred_element_type=F32
    ).astype(BF16)
    gb[y, :, z, c] = block.reshape(4, 32, 256)

    def part(yy, zz, cc):
        return gb.at[yy, :, zz, cc]

    for s in (1, 2, 3):
        send(part(y, z, c), b_send.at[s], b_recv.at[y, z], at_train(y, zplace(s), c))
    for i, d in enumerate(ring):
        send(part(y, z, c), b_send.at[4 + i], b_recv.at[y, z], d)
    send(part(y, z, c), b_send.at[0], b_sib.at[y, z], sib)
    for s in (1, 2, 3):
        zz = zplace(s)
        arrived(part(y, zz, c), b_recv.at[y, zz])
        for i, d in enumerate(ring):
            send(part(y, zz, c), b_send.at[4 + 3 * s + i], b_recv.at[y, zz], d)
        send(part(y, zz, c), b_send.at[15 + s], b_sib.at[y, zz], sib)
    for s in range(4):
        zz = zplace(s)
        for i, yy in enumerate((y_up, y_dn, y_far)):
            arrived(part(yy, zz, c), b_recv.at[yy, zz])
            send(part(yy, zz, c), b_send.at[19 + 3 * s + i], b_sib.at[yy, zz], sib)

    def blocks(h, p):
        side = zh if h == 1 else 1 - zh
        first, second = ((x + 2) % 4, x) if p == 0 else ((x + 1) % 4, (x + 3) % 4)
        return (side * 4 + first) * 128, (side * 4 + second) * 128

    def permute(h, p, yy):
        a, b = blocks(h, p)
        order = order_ref[...]
        j = lax.broadcasted_iota(jnp.int32, (128, 1), 0)
        pick = jnp.concatenate(
            [(order == j + a).astype(F32).astype(BF16), (order == j + b).astype(F32).astype(BF16)], axis=0
        )
        rows = gb[yy].reshape(1024, 256)
        cols = pl.ds(pl.multiple_of(yy * 256, 256), 256)
        ob[2 * h + p, :, cols] = jnp.dot(pick, rows, preferred_element_type=F32).astype(BF16)

    def permute_all(h, p):
        def step(yy, carry):
            permute(h, p, yy)
            return carry
        lax.fori_loop(0, 4, step, 0)

    loads[5].wait()
    for yy in (y, y_up, y_dn, y_far):
        for s in range(4):
            zz = zplace(s)
            arrived(part(yy, zz, 1 - c), b_sib.at[yy, zz])
        permute(0, 0, yy)

    def tile(r, k):
        rows = pl.ds(pl.multiple_of(r * ROWS, ROWS), ROWS)
        t = lax.dot_general(train[rows, :], ob[k], NT, preferred_element_type=F32)
        return t[:, :128] * wcol[r], t[:, 128:] * wcol[r]

    def far_copy(h, i, r, to_right):
        return pltpu.make_async_remote_copy(
            src_ref=s2.at[h, r], dst_ref=(far_l if to_right else far_r).at[h, i], send_sem=s2_send.at[h, r],
            recv_sem=(far_l_recv if to_right else far_r_recv).at[h, i],
            device_id=right if to_right else left, device_id_type=MESH,
        )

    def right_copy(h, r):
        return pltpu.make_async_remote_copy(
            src_ref=sp.at[h, r], dst_ref=got_l.at[h, r], send_sem=sp_send.at[h, r],
            recv_sem=got_l_recv.at[h, r], device_id=right, device_id_type=MESH,
        )

    def left_copy(h, r):
        return pltpu.make_async_remote_copy(
            src_ref=sm.at[h, r], dst_ref=got_r.at[h, r], send_sem=sm_send.at[h, r],
            recv_sem=got_r_recv.at[h, r], device_id=left, device_id_type=MESH,
        )

    def z_copy(r):
        return pltpu.make_async_remote_copy(
            src_ref=zs.at[r], dst_ref=zr.at[r], send_sem=z_send.at[r],
            recv_sem=z_recv.at[r], device_id=across, device_id_type=MESH,
        )

    def out_copy(r):
        rows = pl.ds(pl.multiple_of(r * ROWS, ROWS), ROWS)
        return pltpu.make_async_copy(own.at[1, r], out_ref.at[rows, :], out_sem.at[r])

    def early_copy(half):
        return pltpu.make_async_remote_copy(
            src_ref=s2.at[0, 3 + 4 * half], dst_ref=zf.at[half], send_sem=s2_send.at[0, 3 + 4 * half],
            recv_sem=zf_recv.at[half], device_id=across, device_id_type=MESH,
        )

    def far_blocks(h):
        def step(i, carry):
            for half in (0, 1):
                r = i + 4 * half
                a, b = tile(r, 2 * h)
                s2[h, r] = a.astype(BF16)
                own[h, r] = b
                far_copy(h, i, r, half == 0).start()
            return carry
        lax.fori_loop(0, 3, step, 0)

    def far_last(h):
        for half in (0, 1):
            r = 3 + 4 * half
            a, b = tile(r, 2 * h)
            own[h, r] = b
            if h == 0:
                s2[h, r] = a.astype(BF16)
                early_copy(half).start()
            else:
                early_copy(half).wait_recv()
                s2[h, r] = (a + zf[half].astype(F32)).astype(BF16)
                far_copy(h, 3, r, half == 0).start()

    def near_block(h, i, add):
        p, m = tile(i, 2 * h + 1)
        sm[h, i] = m.astype(BF16)
        left_copy(h, i).start()
        if add:
            far_copy(h, i, i, True).wait_recv()
            p += far_l[h, i].astype(F32)
        sp[h, i] = p.astype(BF16)
        right_copy(h, i).start()
        r = i + 4
        p, m = tile(r, 2 * h + 1)
        sp[h, r] = p.astype(BF16)
        right_copy(h, r).start()
        if add:
            far_copy(h, i, r, False).wait_recv()
            m += far_r[h, i].astype(F32)
        sm[h, r] = m.astype(BF16)
        left_copy(h, r).start()

    def near_blocks(h):
        def step(i, carry):
            near_block(h, i, True)
            return carry
        lax.fori_loop(0, 3 if h == 0 else 4, step, 0)
        if h == 0:
            near_block(h, 3, False)

    def add_up(h, first, last):
        def step(i, carry):
            for half in (0, 1):
                r = i + 4 * half
                right_copy(h, r).wait_recv()
                left_copy(h, r).wait_recv()
                v = own[h, r] + got_l[h, r].astype(F32) + got_r[h, r].astype(F32)
                if h == 0:
                    zs[r] = v.astype(BF16)
                    z_copy(r).start()
                else:
                    z_copy(r).wait_recv()
                    own[1, r] = (v + zr[r].astype(F32)) * 0.125
                    out_copy(r).start()
            return carry
        lax.fori_loop(first, last, step, 0)

    @pl.when(zh == 0)
    def _():
        pl.semaphore_wait(ready, 1)

    far_blocks(0)
    far_last(0)
    permute_all(0, 1)
    near_blocks(0)
    permute_all(1, 0)
    far_blocks(1)
    add_up(0, 0, 1)
    permute_all(1, 1)
    add_up(0, 1, 2)
    far_last(1)
    add_up(0, 2, 4)
    near_blocks(1)
    add_up(1, 0, 4)

    for cp in started:
        cp.wait_send()

    def drain(r, carry):
        for h in (0, 1):
            far_copy(h, 0, r, True).wait_send()
            right_copy(h, r).wait_send()
            left_copy(h, r).wait_send()
        z_copy(r).wait_send()
        out_copy(r).wait()
        return carry
    lax.fori_loop(0, 8, drain, 0)


def shards(train_feat, test_feat, kernel_inv, bucket_weight, bucket, test_order):
    anywhere = pl.BlockSpec(memory_space=pl.ANY)
    vmem = pl.BlockSpec(memory_space=pltpu.VMEM)
    dma = pltpu.SemaphoreType.DMA
    return pl.pallas_call(
        kernel,
        out_shape=jax.ShapeDtypeStruct((2048, 128), F32),
        in_specs=[anywhere] * 6,
        out_specs=pl.BlockSpec(memory_space=pl.ANY),
        scratch_shapes=[
            pltpu.VMEM((1, 16), F32),
            pltpu.VMEM((1, 2048), jnp.int32),
            pltpu.VMEM((1, 1024), jnp.int32),
            pltpu.VMEM((2048, 1024), BF16),
            pltpu.VMEM((4, 32, 1024), BF16),
            pltpu.VMEM((4, 2, 32, 1024), BF16),
            pltpu.VMEM((4, 4, 4, 2, 32, 256), BF16),
            pltpu.VMEM((4, 256, 1024), BF16),
            pltpu.VMEM((8, ROWS, 128), F32),
            pltpu.VMEM((2, 8, ROWS, 128), BF16),
            pltpu.VMEM((2, 8, ROWS, 128), BF16),
            pltpu.VMEM((2, 8, ROWS, 128), BF16),
            pltpu.VMEM((2, 4, ROWS, 128), BF16),
            pltpu.VMEM((2, 4, ROWS, 128), BF16),
            pltpu.VMEM((2, 8, ROWS, 128), BF16),
            pltpu.VMEM((2, 8, ROWS, 128), BF16),
            pltpu.VMEM((2, 8, ROWS, 128), F32),
            pltpu.VMEM((8, ROWS, 128), BF16),
            pltpu.VMEM((8, ROWS, 128), BF16),
            pltpu.VMEM((2, ROWS, 128), BF16),
            pltpu.SemaphoreType.REGULAR,
            dma((8,)),
            dma((6,)),
            dma((3,)),
            dma((4,)),
            dma((7,)),
            dma((4,)),
            dma((4,)),
            dma((31,)),
            dma((4, 4)),
            dma((4, 4)),
            dma((2, 8)),
            dma((2, 8)),
            dma((2, 8)),
            dma((2, 4)),
            dma((2, 4)),
            dma((2, 8)),
            dma((2, 8)),
            dma((8,)),
            dma((8,)),
            dma((2,)),
        ],
        compiler_params=pltpu.CompilerParams(
            collective_id=0, has_side_effects=True, vmem_limit_bytes=60 * 1024 * 1024
        ),
        name="scores",
    )(
        train_feat[0], test_feat[0], kernel_inv[0], bucket_weight,
        bucket.reshape(1, 2048), test_order.reshape(1, 1024),
    )


def solution(mesh):
    return jax.shard_map(
        shards, mesh=mesh,
        in_specs=(P("ckpt", "train", None), P("ckpt", "train", None), P("ckpt", "train", None),
                  P("ckpt", None), P("train"), P(None)),
        out_specs=P("train", "ckpt"), check_vma=False,
    )
```

```python
import functools

import jax
import jax.numpy as jnp
from jax import lax
from jax.experimental import pallas as pl
from jax.experimental.pallas import tpu as pltpu
from jax.sharding import PartitionSpec as P

MESH = pl.DeviceIdType.MESH
F32 = jnp.float32
BF16 = jnp.bfloat16
ROWS = 256
NT = (((1,), (1,)), ((), ()))
TN = (((0,), (0,)), ((), ()))


def kernel(
    train_hbm, test_hbm, kinv_hbm, bw_hbm, bucket_hbm, order_hbm, out_ref,
    bw_ref, bucket_ref, order_ref, train, tb, kb, gb, ob, wcol, s2, sp, sm, far_l, far_r, got_l, got_r, own, zs, zr, zf,
    ready, out_sem, load_sem, t_send, t_recv, k_send, k_recv, k_sib, b_send, b_recv, b_sib, l_send, l_recv, s2_send, sp_send, sm_send,
    far_l_recv, far_r_recv, got_l_recv, got_r_recv, z_send, z_recv, zf_recv,
):
    ck = lax.axis_index("ckpt")
    tr = lax.axis_index("train")
    zh, x = ck // 4, ck % 4
    y, z, c = tr // 8, (tr // 2) % 4, tr % 2

    def at_train(yy, zz, cc):
        return {"ckpt": ck, "train": (yy * 4 + zz) * 2 + cc}

    def at_ckpt(zz, xx):
        return {"ckpt": zz * 4 + xx, "train": tr}

    fold = z // 2
    w = z + fold * (3 - 2 * z)

    def zplace(s):
        if s == 0:
            return z
        v = s - 1 + (s - 1 - w + 4) // 4
        return v + fold * (3 - 2 * v)

    y_up, y_dn, y_far = (y + 1) % 4, (y + 3) % 4, (y + 2) % 4
    up, dn = at_train(y_up, z, c), at_train(y_dn, z, c)
    sib = at_train(y, z, 1 - c)
    right, left = at_ckpt(zh, (x + 1) % 4), at_ckpt(zh, (x + 3) % 4)
    across = at_ckpt(1 - zh, x)

    barrier = pltpu.get_barrier_semaphore()
    partners = [at_train(y, zplace(s), c) for s in (1, 2, 3)]
    partners += [up, dn, at_train(y_far, z, c), right, left, sib]
    for d in partners:
        pl.semaphore_signal(barrier, inc=1, device_id=d, device_id_type=MESH)

    @pl.when(zh == 0)
    def _():
        pl.semaphore_signal(barrier, inc=1, device_id=across, device_id_type=MESH)

    loads = [
        pltpu.make_async_copy(src, dst, load_sem.at[i])
        for i, (src, dst) in enumerate((
            (kinv_hbm, kb.at[z, c]), (test_hbm, tb.at[y]), (bw_hbm, bw_ref),
            (bucket_hbm, bucket_ref), (order_hbm, order_ref), (train_hbm, train),
        ))
    ]
    for cp in loads:
        cp.start()
    pl.semaphore_wait(barrier, len(partners) + zh)

    @pl.when(zh == 1)
    def _():
        pl.semaphore_signal(ready, inc=1, device_id=across, device_id_type=MESH)

    started = []

    def send(ref, send_sem, recv_sem, dev):
        cp = pltpu.make_async_remote_copy(
            src_ref=ref, dst_ref=ref, send_sem=send_sem, recv_sem=recv_sem, device_id=dev, device_id_type=MESH,
        )
        cp.start()
        started.append(cp)

    def arrived(ref, recv_sem):
        pltpu.make_async_remote_copy(
            src_ref=ref, dst_ref=ref, send_sem=b_send.at[0], recv_sem=recv_sem, device_id=sib, device_id_type=MESH,
        ).wait_recv()

    ring = [at_train(y_far, z, c), up, dn]

    loads[0].wait()
    for s in (1, 2, 3):
        send(kb.at[z, c], k_send.at[s], k_recv.at[z], at_train(y, zplace(s), c))
    send(kb.at[z, c], k_send.at[0], k_sib.at[z], sib)
    loads[1].wait()
    for i, d in enumerate(ring):
        send(tb.at[y], t_send.at[i], t_recv.at[y], d)

    for i in (2, 3, 4):
        loads[i].wait()

    eye = lax.broadcasted_iota(jnp.int32, (16, 16), 0) == lax.broadcasted_iota(jnp.int32, (16, 16), 1)
    col = jnp.sum(jnp.where(eye, jnp.broadcast_to(bw_ref[...], (16, 16)), 0.0), axis=1, keepdims=True)
    col = jnp.broadcast_to(col, (16, 128))
    hi = col.astype(BF16)
    rest = col - hi.astype(F32)
    mid = rest.astype(BF16)
    low = (rest - mid.astype(F32)).astype(BF16)

    def weigh(i, carry):
        rows = pl.ds(pl.multiple_of(i * ROWS, ROWS), ROWS)
        b = bucket_ref[:, rows]
        hot = (lax.broadcasted_iota(jnp.int32, (16, 1), 0) == b).astype(F32).astype(BF16)
        acc = lax.dot_general(hot, hi, TN, preferred_element_type=F32)
        acc += lax.dot_general(hot, mid, TN, preferred_element_type=F32)
        acc += lax.dot_general(hot, low, TN, preferred_element_type=F32)
        wcol[i] = acc
        return carry
    lax.fori_loop(0, 8, weigh, 0)

    for s in (1, 2, 3):
        zz = zplace(s)
        arrived(kb.at[zz, c], k_recv.at[zz])
        send(kb.at[zz, c], k_send.at[3 + s], k_sib.at[zz], sib)
    for yy in (y_up, y_dn, y_far):
        arrived(tb.at[yy], t_recv.at[yy])
    for s in range(4):
        zz = zplace(s)
        arrived(kb.at[zz, 1 - c], k_sib.at[zz])

    block = lax.dot_general(
        tb[...].reshape(128, 1024), kb[...].reshape(256, 1024), NT, preferred_element_type=F32
    ).astype(BF16)
    gb[y, :, z, c] = block.reshape(4, 32, 256)

    def part(yy, zz, cc):
        return gb.at[yy, :, zz, cc]

    for s in (1, 2, 3):
        send(part(y, z, c), b_send.at[s], b_recv.at[y, z], at_train(y, zplace(s), c))
    for i, d in enumerate(ring):
        send(part(y, z, c), b_send.at[4 + i], b_recv.at[y, z], d)
    send(part(y, z, c), b_send.at[0], b_sib.at[y, z], sib)
    def most(yy, zz):
        return gb.at[yy, pl.ds(0, 3), zz, c]

    def last(yy, zz):
        return gb.at[yy, 3, zz, c]

    def from_line(s):
        zz = zplace(s)
        arrived(part(y, zz, c), b_recv.at[y, zz])
        for i, d in enumerate(ring):
            send(most(y, zz), b_send.at[4 + 3 * s + i], b_recv.at[y, zz], d)
        send(part(y, zz, c), b_send.at[15 + s], b_sib.at[y, zz], sib)

    from_line(1)
    from_line(2)
    for i, yy in enumerate((y_up, y_dn, y_far)):
        arrived(part(yy, z, c), b_recv.at[yy, z])
        for s in (1, 2, 3):
            send(last(yy, z), l_send.at[3 * i + s - 1], l_recv.at[yy, z], at_train(y, zplace(s), c))
        send(part(yy, z, c), b_send.at[19 + i], b_sib.at[yy, z], sib)
    from_line(3)
    for s in (1, 2, 3):
        zz = zplace(s)
        for i, yy in enumerate((y_up, y_dn, y_far)):
            arrived(most(yy, zz), b_recv.at[yy, zz])
            arrived(last(yy, zz), l_recv.at[yy, zz])
            send(part(yy, zz, c), b_send.at[19 + 3 * s + i], b_sib.at[yy, zz], sib)

    def blocks(h, p):
        side = zh if h == 1 else 1 - zh
        first, second = ((x + 2) % 4, x) if p == 0 else ((x + 1) % 4, (x + 3) % 4)
        return (side * 4 + first) * 128, (side * 4 + second) * 128

    def permute(h, p, yy):
        a, b = blocks(h, p)
        order = order_ref[...]
        j = lax.broadcasted_iota(jnp.int32, (128, 1), 0)
        pick = jnp.concatenate(
            [(order == j + a).astype(F32).astype(BF16), (order == j + b).astype(F32).astype(BF16)], axis=0
        )
        rows = gb[yy].reshape(1024, 256)
        cols = pl.ds(pl.multiple_of(yy * 256, 256), 256)
        ob[2 * h + p, :, cols] = jnp.dot(pick, rows, preferred_element_type=F32).astype(BF16)

    def permute_all(h, p):
        def step(yy, carry):
            permute(h, p, yy)
            return carry
        lax.fori_loop(0, 4, step, 0)

    loads[5].wait()
    for yy in (y, y_up, y_dn, y_far):
        for s in range(4):
            zz = zplace(s)
            arrived(part(yy, zz, 1 - c), b_sib.at[yy, zz])
        permute(0, 0, yy)

    def tile(r, k):
        rows = pl.ds(pl.multiple_of(r * ROWS, ROWS), ROWS)
        t = lax.dot_general(train[rows, :], ob[k], NT, preferred_element_type=F32)
        return t[:, :128] * wcol[r], t[:, 128:] * wcol[r]

    def far_copy(h, i, r, to_right):
        return pltpu.make_async_remote_copy(
            src_ref=s2.at[h, r], dst_ref=(far_l if to_right else far_r).at[h, i], send_sem=s2_send.at[h, r],
            recv_sem=(far_l_recv if to_right else far_r_recv).at[h, i],
            device_id=right if to_right else left, device_id_type=MESH,
        )

    def right_copy(h, r):
        return pltpu.make_async_remote_copy(
            src_ref=sp.at[h, r], dst_ref=got_l.at[h, r], send_sem=sp_send.at[h, r],
            recv_sem=got_l_recv.at[h, r], device_id=right, device_id_type=MESH,
        )

    def left_copy(h, r):
        return pltpu.make_async_remote_copy(
            src_ref=sm.at[h, r], dst_ref=got_r.at[h, r], send_sem=sm_send.at[h, r],
            recv_sem=got_r_recv.at[h, r], device_id=left, device_id_type=MESH,
        )

    def z_copy(r):
        return pltpu.make_async_remote_copy(
            src_ref=zs.at[r], dst_ref=zr.at[r], send_sem=z_send.at[r],
            recv_sem=z_recv.at[r], device_id=across, device_id_type=MESH,
        )

    def out_copy(r):
        rows = pl.ds(pl.multiple_of(r * ROWS, ROWS), ROWS)
        return pltpu.make_async_copy(own.at[1, r], out_ref.at[rows, :], out_sem.at[r])

    def early_copy(half):
        return pltpu.make_async_remote_copy(
            src_ref=s2.at[0, 3 + 4 * half], dst_ref=zf.at[half], send_sem=s2_send.at[0, 3 + 4 * half],
            recv_sem=zf_recv.at[half], device_id=across, device_id_type=MESH,
        )

    def far_blocks(h, first, last):
        def step(i, carry):
            for half in (0, 1):
                r = i + 4 * half
                a, b = tile(r, 2 * h)
                s2[h, r] = a.astype(BF16)
                own[h, r] = b
                far_copy(h, i, r, half == 0).start()
            return carry
        lax.fori_loop(first, last, step, 0)

    def far_last(h):
        for half in (0, 1):
            r = 3 + 4 * half
            a, b = tile(r, 2 * h)
            own[h, r] = b
            if h == 0:
                s2[h, r] = a.astype(BF16)
                early_copy(half).start()
            else:
                early_copy(half).wait_recv()
                s2[h, r] = (a + zf[half].astype(F32)).astype(BF16)
                far_copy(h, 3, r, half == 0).start()

    def near_block(h, i, add):
        p, m = tile(i, 2 * h + 1)
        sm[h, i] = m.astype(BF16)
        left_copy(h, i).start()
        if add:
            far_copy(h, i, i, True).wait_recv()
            p += far_l[h, i].astype(F32)
        sp[h, i] = p.astype(BF16)
        right_copy(h, i).start()
        r = i + 4
        p, m = tile(r, 2 * h + 1)
        sp[h, r] = p.astype(BF16)
        right_copy(h, r).start()
        if add:
            far_copy(h, i, r, False).wait_recv()
            m += far_r[h, i].astype(F32)
        sm[h, r] = m.astype(BF16)
        left_copy(h, r).start()

    def near_blocks(h, first, last):
        def step(i, carry):
            near_block(h, i, True)
            return carry
        lax.fori_loop(first, last, step, 0)

    def add_up(h, first, last):
        def step(i, carry):
            for half in (0, 1):
                r = i + 4 * half
                right_copy(h, r).wait_recv()
                left_copy(h, r).wait_recv()
                v = own[h, r] + got_l[h, r].astype(F32) + got_r[h, r].astype(F32)
                if h == 0:
                    zs[r] = v.astype(BF16)
                    z_copy(r).start()
                else:
                    z_copy(r).wait_recv()
                    own[1, r] = (v + zr[r].astype(F32)) * 0.125
                    out_copy(r).start()
            return carry
        lax.fori_loop(first, last, step, 0)

    @pl.when(zh == 0)
    def _():
        pl.semaphore_wait(ready, 1)

    far_blocks(0, 0, 1)
    far_last(0)
    far_blocks(0, 1, 2)
    permute_all(0, 1)
    near_block(0, 3, False)
    far_blocks(0, 2, 3)
    near_blocks(0, 0, 2)
    permute_all(1, 0)
    add_up(0, 3, 4)
    near_blocks(0, 2, 3)
    far_blocks(1, 0, 3)
    add_up(0, 0, 1)
    permute_all(1, 1)
    add_up(0, 1, 2)
    far_last(1)
    add_up(0, 2, 3)
    near_blocks(1, 0, 4)
    add_up(1, 0, 4)

    for cp in started:
        cp.wait_send()

    def drain(r, carry):
        for h in (0, 1):
            far_copy(h, 0, r, True).wait_send()
            right_copy(h, r).wait_send()
            left_copy(h, r).wait_send()
        z_copy(r).wait_send()
        out_copy(r).wait()
        return carry
    lax.fori_loop(0, 8, drain, 0)


def shards(train_feat, test_feat, kernel_inv, bucket_weight, bucket, test_order):
    anywhere = pl.BlockSpec(memory_space=pl.ANY)
    vmem = pl.BlockSpec(memory_space=pltpu.VMEM)
    dma = pltpu.SemaphoreType.DMA
    return pl.pallas_call(
        kernel,
        out_shape=jax.ShapeDtypeStruct((2048, 128), F32),
        in_specs=[anywhere] * 6,
        out_specs=pl.BlockSpec(memory_space=pl.ANY),
        scratch_shapes=[
            pltpu.VMEM((1, 16), F32),
            pltpu.VMEM((1, 2048), jnp.int32),
            pltpu.VMEM((1, 1024), jnp.int32),
            pltpu.VMEM((2048, 1024), BF16),
            pltpu.VMEM((4, 32, 1024), BF16),
            pltpu.VMEM((4, 2, 32, 1024), BF16),
            pltpu.VMEM((4, 4, 4, 2, 32, 256), BF16),
            pltpu.VMEM((4, 256, 1024), BF16),
            pltpu.VMEM((8, ROWS, 128), F32),
            pltpu.VMEM((2, 8, ROWS, 128), BF16),
            pltpu.VMEM((2, 8, ROWS, 128), BF16),
            pltpu.VMEM((2, 8, ROWS, 128), BF16),
            pltpu.VMEM((2, 4, ROWS, 128), BF16),
            pltpu.VMEM((2, 4, ROWS, 128), BF16),
            pltpu.VMEM((2, 8, ROWS, 128), BF16),
            pltpu.VMEM((2, 8, ROWS, 128), BF16),
            pltpu.VMEM((2, 8, ROWS, 128), F32),
            pltpu.VMEM((8, ROWS, 128), BF16),
            pltpu.VMEM((8, ROWS, 128), BF16),
            pltpu.VMEM((2, ROWS, 128), BF16),
            pltpu.SemaphoreType.REGULAR,
            dma((8,)),
            dma((6,)),
            dma((3,)),
            dma((4,)),
            dma((7,)),
            dma((4,)),
            dma((4,)),
            dma((31,)),
            dma((4, 4)),
            dma((4, 4)),
            dma((9,)),
            dma((4, 4)),
            dma((2, 8)),
            dma((2, 8)),
            dma((2, 8)),
            dma((2, 4)),
            dma((2, 4)),
            dma((2, 8)),
            dma((2, 8)),
            dma((8,)),
            dma((8,)),
            dma((2,)),
        ],
        compiler_params=pltpu.CompilerParams(
            collective_id=0, has_side_effects=True, vmem_limit_bytes=60 * 1024 * 1024
        ),
        name="scores",
    )(
        train_feat[0], test_feat[0], kernel_inv[0], bucket_weight,
        bucket.reshape(1, 2048), test_order.reshape(1, 1024),
    )


def solution(mesh):
    return jax.shard_map(
        shards, mesh=mesh,
        in_specs=(P("ckpt", "train", None), P("ckpt", "train", None), P("ckpt", "train", None),
                  P("ckpt", None), P("train"), P(None)),
        out_specs=P("train", "ckpt"), check_vma=False,
    )
```

```python
import functools

import jax
import jax.numpy as jnp
from jax import lax
from jax.experimental import pallas as pl
from jax.experimental.pallas import tpu as pltpu
from jax.sharding import PartitionSpec as P

MESH = pl.DeviceIdType.MESH
F32 = jnp.float32
BF16 = jnp.bfloat16
ROWS = 256
NT = (((1,), (1,)), ((), ()))
TN = (((0,), (0,)), ((), ()))


def kernel(
    train_hbm, test_hbm, kinv_hbm, bw_hbm, bucket_hbm, order_hbm, out_ref,
    bw_ref, bucket_ref, order_ref, by_place, train, tb, kb, gb, ob, wcol, s2, sp, sm, far_l, far_r, got_l, got_r, own, zs, zr, zf,
    ready, out_sem, load_sem, t_send, t_recv, k_send, k_recv, k_sib, b_send, b_recv, b_sib, l_send, l_recv, s2_send, sp_send, sm_send,
    far_l_recv, far_r_recv, got_l_recv, got_r_recv, z_send, z_recv, zf_recv,
):
    ck = lax.axis_index("ckpt")
    tr = lax.axis_index("train")
    zh, x = ck // 4, ck % 4
    y, z, c = tr // 8, (tr // 2) % 4, tr % 2

    def at_train(yy, zz, cc):
        return {"ckpt": ck, "train": (yy * 4 + zz) * 2 + cc}

    def at_ckpt(zz, xx):
        return {"ckpt": zz * 4 + xx, "train": tr}

    fold = z // 2
    w = z + fold * (3 - 2 * z)

    def zplace(s):
        if s == 0:
            return z
        v = s - 1 + (s - 1 - w + 4) // 4
        return v + fold * (3 - 2 * v)

    y_up, y_dn, y_far = (y + 1) % 4, (y + 3) % 4, (y + 2) % 4
    up, dn = at_train(y_up, z, c), at_train(y_dn, z, c)
    sib = at_train(y, z, 1 - c)
    right, left = at_ckpt(zh, (x + 1) % 4), at_ckpt(zh, (x + 3) % 4)
    across = at_ckpt(1 - zh, x)

    barrier = pltpu.get_barrier_semaphore()
    partners = [at_train(y, zplace(s), c) for s in (1, 2, 3)]
    partners += [up, dn, at_train(y_far, z, c), right, left, sib]
    for d in partners:
        pl.semaphore_signal(barrier, inc=1, device_id=d, device_id_type=MESH)

    @pl.when(zh == 0)
    def _():
        pl.semaphore_signal(barrier, inc=1, device_id=across, device_id_type=MESH)

    loads = [
        pltpu.make_async_copy(src, dst, load_sem.at[i])
        for i, (src, dst) in enumerate((
            (kinv_hbm, kb.at[z, c]), (test_hbm, tb.at[y]), (bw_hbm, bw_ref),
            (bucket_hbm, bucket_ref), (order_hbm, order_ref), (train_hbm, train),
        ))
    ]
    for cp in loads:
        cp.start()
    pl.semaphore_wait(barrier, len(partners) + zh)

    @pl.when(zh == 1)
    def _():
        pl.semaphore_signal(ready, inc=1, device_id=across, device_id_type=MESH)

    started = []

    def send(ref, send_sem, recv_sem, dev):
        cp = pltpu.make_async_remote_copy(
            src_ref=ref, dst_ref=ref, send_sem=send_sem, recv_sem=recv_sem, device_id=dev, device_id_type=MESH,
        )
        cp.start()
        started.append(cp)

    def arrived(ref, recv_sem):
        pltpu.make_async_remote_copy(
            src_ref=ref, dst_ref=ref, send_sem=b_send.at[0], recv_sem=recv_sem, device_id=sib, device_id_type=MESH,
        ).wait_recv()

    ring = [at_train(y_far, z, c), up, dn]

    loads[0].wait()
    for s in (1, 2, 3):
        send(kb.at[z, c], k_send.at[s], k_recv.at[z], at_train(y, zplace(s), c))
    send(kb.at[z, c], k_send.at[0], k_sib.at[z], sib)
    loads[1].wait()
    for i, d in enumerate(ring):
        send(tb.at[y], t_send.at[i], t_recv.at[y], d)

    for i in (2, 3, 4):
        loads[i].wait()

    order = order_ref[...]
    by_place[...] = jnp.concatenate(
        [order[:, 256 * i + 64 * k:256 * i + 64 * k + 64] for k in range(4) for i in range(4)], axis=1
    )

    eye = lax.broadcasted_iota(jnp.int32, (16, 16), 0) == lax.broadcasted_iota(jnp.int32, (16, 16), 1)
    col = jnp.sum(jnp.where(eye, jnp.broadcast_to(bw_ref[...], (16, 16)), 0.0), axis=1, keepdims=True)
    col = jnp.broadcast_to(col, (16, 128))
    hi = col.astype(BF16)
    rest = col - hi.astype(F32)
    mid = rest.astype(BF16)
    low = (rest - mid.astype(F32)).astype(BF16)

    def weigh(i, carry):
        rows = pl.ds(pl.multiple_of(i * ROWS, ROWS), ROWS)
        b = bucket_ref[:, rows]
        hot = (lax.broadcasted_iota(jnp.int32, (16, 1), 0) == b).astype(F32).astype(BF16)
        acc = lax.dot_general(hot, hi, TN, preferred_element_type=F32)
        acc += lax.dot_general(hot, mid, TN, preferred_element_type=F32)
        acc += lax.dot_general(hot, low, TN, preferred_element_type=F32)
        wcol[i] = acc
        return carry
    lax.fori_loop(0, 8, weigh, 0)

    for s in (1, 2, 3):
        zz = zplace(s)
        arrived(kb.at[zz, c], k_recv.at[zz])
        send(kb.at[zz, c], k_send.at[3 + s], k_sib.at[zz], sib)
    for yy in (y_up, y_dn, y_far):
        arrived(tb.at[yy], t_recv.at[yy])
    for s in range(4):
        zz = zplace(s)
        arrived(kb.at[zz, 1 - c], k_sib.at[zz])

    block = lax.dot_general(
        tb[...].reshape(128, 1024), kb[...].reshape(256, 1024), NT, preferred_element_type=F32
    ).astype(BF16)
    gb[y, :, z, c] = block.reshape(4, 32, 256)

    def part(yy, zz, cc):
        return gb.at[yy, :, zz, cc]

    for s in (1, 2, 3):
        send(part(y, z, c), b_send.at[s], b_recv.at[y, z], at_train(y, zplace(s), c))
    for i, d in enumerate(ring):
        send(part(y, z, c), b_send.at[4 + i], b_recv.at[y, z], d)
    send(part(y, z, c), b_send.at[0], b_sib.at[y, z], sib)
    def most(yy, zz):
        return gb.at[yy, pl.ds(0, 3), zz, c]

    def last(yy, zz):
        return gb.at[yy, 3, zz, c]

    def from_line(s):
        zz = zplace(s)
        arrived(part(y, zz, c), b_recv.at[y, zz])
        for i, d in enumerate(ring):
            send(most(y, zz), b_send.at[4 + 3 * s + i], b_recv.at[y, zz], d)
        send(part(y, zz, c), b_send.at[15 + s], b_sib.at[y, zz], sib)

    from_line(1)
    from_line(2)
    for i, yy in enumerate((y_up, y_dn, y_far)):
        arrived(part(yy, z, c), b_recv.at[yy, z])
        for s in (1, 2, 3):
            send(last(yy, z), l_send.at[3 * i + s - 1], l_recv.at[yy, z], at_train(y, zplace(s), c))
        send(part(yy, z, c), b_send.at[19 + i], b_sib.at[yy, z], sib)
    from_line(3)
    for s in (1, 2, 3):
        zz = zplace(s)
        for i, yy in enumerate((y_up, y_dn, y_far)):
            arrived(most(yy, zz), b_recv.at[yy, zz])
            arrived(last(yy, zz), l_recv.at[yy, zz])
            send(part(yy, zz, c), b_send.at[19 + 3 * s + i], b_sib.at[yy, zz], sib)

    def blocks(h, p):
        side = zh if h == 1 else 1 - zh
        first, second = ((x + 2) % 4, x) if p == 0 else ((x + 1) % 4, (x + 3) % 4)
        return (side * 4 + first) * 128, (side * 4 + second) * 128

    def permute(h, p, yy):
        a, b = blocks(h, p)
        order = order_ref[...]
        j = lax.broadcasted_iota(jnp.int32, (128, 1), 0)
        pick = jnp.concatenate(
            [(order == j + a).astype(F32).astype(BF16), (order == j + b).astype(F32).astype(BF16)], axis=0
        )
        rows = gb[yy].reshape(1024, 256)
        cols = pl.ds(pl.multiple_of(yy * 256, 256), 256)
        ob[2 * h + p, :, cols] = jnp.dot(pick, rows, preferred_element_type=F32).astype(BF16)

    def permute_all(h, p):
        def step(yy, carry):
            permute(h, p, yy)
            return carry
        lax.fori_loop(0, 4, step, 0)

    first_a, first_b = blocks(0, 0)
    j = lax.broadcasted_iota(jnp.int32, (128, 1), 0)

    def permute_from(zz, fresh):
        order = by_place[:, pl.ds(pl.multiple_of(zz * 256, 256), 256)]
        pick = jnp.concatenate(
            [(order == j + first_a).astype(F32).astype(BF16), (order == j + first_b).astype(F32).astype(BF16)], axis=0
        )
        for yy in range(4):
            cols = pl.ds(yy * 256, 256)
            got = jnp.dot(pick, gb[yy, :, zz].reshape(256, 256), preferred_element_type=F32).astype(BF16)
            ob[0, :, cols] = got if fresh else ob[0, :, cols] + got

    loads[5].wait()
    for s in range(4):
        zz = zplace(s)
        for yy in (y, y_up, y_dn, y_far):
            arrived(part(yy, zz, 1 - c), b_sib.at[yy, zz])
        permute_from(zz, s == 0)

    def tile(r, k):
        rows = pl.ds(pl.multiple_of(r * ROWS, ROWS), ROWS)
        t = lax.dot_general(train[rows, :], ob[k], NT, preferred_element_type=F32)
        return t[:, :128] * wcol[r], t[:, 128:] * wcol[r]

    def far_copy(h, i, r, to_right):
        return pltpu.make_async_remote_copy(
            src_ref=s2.at[h, r], dst_ref=(far_l if to_right else far_r).at[h, i], send_sem=s2_send.at[h, r],
            recv_sem=(far_l_recv if to_right else far_r_recv).at[h, i],
            device_id=right if to_right else left, device_id_type=MESH,
        )

    def right_copy(h, r):
        return pltpu.make_async_remote_copy(
            src_ref=sp.at[h, r], dst_ref=got_l.at[h, r], send_sem=sp_send.at[h, r],
            recv_sem=got_l_recv.at[h, r], device_id=right, device_id_type=MESH,
        )

    def left_copy(h, r):
        return pltpu.make_async_remote_copy(
            src_ref=sm.at[h, r], dst_ref=got_r.at[h, r], send_sem=sm_send.at[h, r],
            recv_sem=got_r_recv.at[h, r], device_id=left, device_id_type=MESH,
        )

    def z_copy(r):
        return pltpu.make_async_remote_copy(
            src_ref=zs.at[r], dst_ref=zr.at[r], send_sem=z_send.at[r],
            recv_sem=z_recv.at[r], device_id=across, device_id_type=MESH,
        )

    def out_copy(r):
        rows = pl.ds(pl.multiple_of(r * ROWS, ROWS), ROWS)
        return pltpu.make_async_copy(own.at[1, r], out_ref.at[rows, :], out_sem.at[r])

    def early_copy(half):
        return pltpu.make_async_remote_copy(
            src_ref=s2.at[0, 3 + 4 * half], dst_ref=zf.at[half], send_sem=s2_send.at[0, 3 + 4 * half],
            recv_sem=zf_recv.at[half], device_id=across, device_id_type=MESH,
        )

    def far_blocks(h, first, last):
        def step(i, carry):
            for half in (0, 1):
                r = i + 4 * half
                a, b = tile(r, 2 * h)
                s2[h, r] = a.astype(BF16)
                own[h, r] = b
                far_copy(h, i, r, half == 0).start()
            return carry
        lax.fori_loop(first, last, step, 0)

    def far_last(h):
        for half in (0, 1):
            r = 3 + 4 * half
            a, b = tile(r, 2 * h)
            own[h, r] = b
            if h == 0:
                s2[h, r] = a.astype(BF16)
                early_copy(half).start()
            else:
                early_copy(half).wait_recv()
                s2[h, r] = (a + zf[half].astype(F32)).astype(BF16)
                far_copy(h, 3, r, half == 0).start()

    def near_block(h, i, add):
        p, m = tile(i, 2 * h + 1)
        sm[h, i] = m.astype(BF16)
        left_copy(h, i).start()
        if add:
            far_copy(h, i, i, True).wait_recv()
            p += far_l[h, i].astype(F32)
        sp[h, i] = p.astype(BF16)
        right_copy(h, i).start()
        r = i + 4
        p, m = tile(r, 2 * h + 1)
        sp[h, r] = p.astype(BF16)
        right_copy(h, r).start()
        if add:
            far_copy(h, i, r, False).wait_recv()
            m += far_r[h, i].astype(F32)
        sm[h, r] = m.astype(BF16)
        left_copy(h, r).start()

    def near_blocks(h, first, last):
        def step(i, carry):
            near_block(h, i, True)
            return carry
        lax.fori_loop(first, last, step, 0)

    def add_up(h, first, last):
        def step(i, carry):
            for half in (0, 1):
                r = i + 4 * half
                right_copy(h, r).wait_recv()
                left_copy(h, r).wait_recv()
                v = own[h, r] + got_l[h, r].astype(F32) + got_r[h, r].astype(F32)
                if h == 0:
                    zs[r] = v.astype(BF16)
                    z_copy(r).start()
                else:
                    z_copy(r).wait_recv()
                    own[1, r] = (v + zr[r].astype(F32)) * 0.125
                    out_copy(r).start()
            return carry
        lax.fori_loop(first, last, step, 0)

    @pl.when(zh == 0)
    def _():
        pl.semaphore_wait(ready, 1)

    far_blocks(0, 0, 1)
    far_last(0)
    far_blocks(0, 1, 2)
    permute_all(0, 1)
    near_block(0, 3, False)
    far_blocks(0, 2, 3)
    near_blocks(0, 0, 2)
    permute_all(1, 0)
    add_up(0, 3, 4)
    near_blocks(0, 2, 3)
    far_blocks(1, 0, 3)
    add_up(0, 0, 1)
    permute_all(1, 1)
    add_up(0, 1, 2)
    far_last(1)
    add_up(0, 2, 3)
    near_blocks(1, 0, 4)
    add_up(1, 0, 4)

    for cp in started:
        cp.wait_send()

    def drain(r, carry):
        for h in (0, 1):
            far_copy(h, 0, r, True).wait_send()
            right_copy(h, r).wait_send()
            left_copy(h, r).wait_send()
        z_copy(r).wait_send()
        out_copy(r).wait()
        return carry
    lax.fori_loop(0, 8, drain, 0)


def shards(train_feat, test_feat, kernel_inv, bucket_weight, bucket, test_order):
    anywhere = pl.BlockSpec(memory_space=pl.ANY)
    vmem = pl.BlockSpec(memory_space=pltpu.VMEM)
    dma = pltpu.SemaphoreType.DMA
    return pl.pallas_call(
        kernel,
        out_shape=jax.ShapeDtypeStruct((2048, 128), F32),
        in_specs=[anywhere] * 6,
        out_specs=pl.BlockSpec(memory_space=pl.ANY),
        scratch_shapes=[
            pltpu.VMEM((1, 16), F32),
            pltpu.VMEM((1, 2048), jnp.int32),
            pltpu.VMEM((1, 1024), jnp.int32),
            pltpu.VMEM((1, 1024), jnp.int32),
            pltpu.VMEM((2048, 1024), BF16),
            pltpu.VMEM((4, 32, 1024), BF16),
            pltpu.VMEM((4, 2, 32, 1024), BF16),
            pltpu.VMEM((4, 4, 4, 2, 32, 256), BF16),
            pltpu.VMEM((4, 256, 1024), BF16),
            pltpu.VMEM((8, ROWS, 128), F32),
            pltpu.VMEM((2, 8, ROWS, 128), BF16),
            pltpu.VMEM((2, 8, ROWS, 128), BF16),
            pltpu.VMEM((2, 8, ROWS, 128), BF16),
            pltpu.VMEM((2, 4, ROWS, 128), BF16),
            pltpu.VMEM((2, 4, ROWS, 128), BF16),
            pltpu.VMEM((2, 8, ROWS, 128), BF16),
            pltpu.VMEM((2, 8, ROWS, 128), BF16),
            pltpu.VMEM((2, 8, ROWS, 128), F32),
            pltpu.VMEM((8, ROWS, 128), BF16),
            pltpu.VMEM((8, ROWS, 128), BF16),
            pltpu.VMEM((2, ROWS, 128), BF16),
            pltpu.SemaphoreType.REGULAR,
            dma((8,)),
            dma((6,)),
            dma((3,)),
            dma((4,)),
            dma((7,)),
            dma((4,)),
            dma((4,)),
            dma((31,)),
            dma((4, 4)),
            dma((4, 4)),
            dma((9,)),
            dma((4, 4)),
            dma((2, 8)),
            dma((2, 8)),
            dma((2, 8)),
            dma((2, 4)),
            dma((2, 4)),
            dma((2, 8)),
            dma((2, 8)),
            dma((8,)),
            dma((8,)),
            dma((2,)),
        ],
        compiler_params=pltpu.CompilerParams(
            collective_id=0, has_side_effects=True, vmem_limit_bytes=60 * 1024 * 1024
        ),
        name="scores",
    )(
        train_feat[0], test_feat[0], kernel_inv[0], bucket_weight,
        bucket.reshape(1, 2048), test_order.reshape(1, 1024),
    )


def solution(mesh):
    return jax.shard_map(
        shards, mesh=mesh,
        in_specs=(P("ckpt", "train", None), P("ckpt", "train", None), P("ckpt", "train", None),
                  P("ckpt", None), P("train"), P(None)),
        out_specs=P("train", "ckpt"), check_vma=False,
    )
```

```python
import functools

import jax
import jax.numpy as jnp
from jax import lax
from jax.experimental import pallas as pl
from jax.experimental.pallas import tpu as pltpu
from jax.sharding import PartitionSpec as P

MESH = pl.DeviceIdType.MESH
F32 = jnp.float32
BF16 = jnp.bfloat16
ROWS = 256
NT = (((1,), (1,)), ((), ()))
TN = (((0,), (0,)), ((), ()))


def kernel(
    train_hbm, test_hbm, kinv_hbm, bw_hbm, bucket_hbm, order_hbm, out_ref,
    bw_ref, bucket_ref, order_ref, by_place, train, tb, kb, gb, ob, wcol, s2, sp, sm, far_l, far_r, got_l, got_r, own, zs, zr, zf,
    ready, out_sem, load_sem, t_send, t_recv, k_send, k_recv, k_sib, b_send, b_recv, b_sib, l_send, l_recv, s2_send, sp_send, sm_send,
    far_l_recv, far_r_recv, got_l_recv, got_r_recv, z_send, z_recv, zf_recv,
):
    ck = lax.axis_index("ckpt")
    tr = lax.axis_index("train")
    zh, x = ck // 4, ck % 4
    y, z, c = tr // 8, (tr // 2) % 4, tr % 2

    def at_train(yy, zz, cc):
        return {"ckpt": ck, "train": (yy * 4 + zz) * 2 + cc}

    def at_ckpt(zz, xx):
        return {"ckpt": zz * 4 + xx, "train": tr}

    fold = z // 2
    w = z + fold * (3 - 2 * z)

    def zplace(s):
        if s == 0:
            return z
        v = s - 1 + (s - 1 - w + 4) // 4
        return v + fold * (3 - 2 * v)

    y_up, y_dn, y_far = (y + 1) % 4, (y + 3) % 4, (y + 2) % 4
    up, dn = at_train(y_up, z, c), at_train(y_dn, z, c)
    sib = at_train(y, z, 1 - c)
    right, left = at_ckpt(zh, (x + 1) % 4), at_ckpt(zh, (x + 3) % 4)
    across = at_ckpt(1 - zh, x)

    barrier = pltpu.get_barrier_semaphore()
    partners = [at_train(y, zplace(s), c) for s in (1, 2, 3)]
    partners += [up, dn, at_train(y_far, z, c), right, left, sib]
    for d in partners:
        pl.semaphore_signal(barrier, inc=1, device_id=d, device_id_type=MESH)

    @pl.when(zh == 0)
    def _():
        pl.semaphore_signal(barrier, inc=1, device_id=across, device_id_type=MESH)

    loads = [
        pltpu.make_async_copy(src, dst, load_sem.at[i])
        for i, (src, dst) in enumerate((
            (kinv_hbm, kb.at[z, c]), (test_hbm, tb.at[y]), (bw_hbm, bw_ref),
            (bucket_hbm, bucket_ref), (order_hbm, order_ref), (train_hbm, train),
        ))
    ]
    for cp in loads:
        cp.start()
    pl.semaphore_wait(barrier, len(partners) + zh)

    @pl.when(zh == 1)
    def _():
        pl.semaphore_signal(ready, inc=1, device_id=across, device_id_type=MESH)

    started = []

    def send(ref, send_sem, recv_sem, dev):
        cp = pltpu.make_async_remote_copy(
            src_ref=ref, dst_ref=ref, send_sem=send_sem, recv_sem=recv_sem, device_id=dev, device_id_type=MESH,
        )
        cp.start()
        started.append(cp)

    def arrived(ref, recv_sem):
        pltpu.make_async_remote_copy(
            src_ref=ref, dst_ref=ref, send_sem=b_send.at[0], recv_sem=recv_sem, device_id=sib, device_id_type=MESH,
        ).wait_recv()

    ring = [up, dn, at_train(y_far, z, c)]

    loads[0].wait()
    for s in (1, 2, 3):
        send(kb.at[z, c], k_send.at[s], k_recv.at[z], at_train(y, zplace(s), c))
    send(kb.at[z, c], k_send.at[0], k_sib.at[z], sib)
    loads[1].wait()
    for i, d in enumerate(ring):
        send(tb.at[y], t_send.at[i], t_recv.at[y], d)

    for i in (2, 3, 4):
        loads[i].wait()

    order = order_ref[...]
    by_place[...] = jnp.concatenate(
        [order[:, 256 * i + 64 * k:256 * i + 64 * k + 64] for k in range(4) for i in range(4)], axis=1
    )

    eye = lax.broadcasted_iota(jnp.int32, (16, 16), 0) == lax.broadcasted_iota(jnp.int32, (16, 16), 1)
    col = jnp.sum(jnp.where(eye, jnp.broadcast_to(bw_ref[...], (16, 16)), 0.0), axis=1, keepdims=True)
    col = jnp.broadcast_to(col, (16, 128))
    hi = col.astype(BF16)
    rest = col - hi.astype(F32)
    mid = rest.astype(BF16)
    low = (rest - mid.astype(F32)).astype(BF16)

    def weigh(i, carry):
        rows = pl.ds(pl.multiple_of(i * ROWS, ROWS), ROWS)
        b = bucket_ref[:, rows]
        hot = (lax.broadcasted_iota(jnp.int32, (16, 1), 0) == b).astype(F32).astype(BF16)
        acc = lax.dot_general(hot, hi, TN, preferred_element_type=F32)
        acc += lax.dot_general(hot, mid, TN, preferred_element_type=F32)
        acc += lax.dot_general(hot, low, TN, preferred_element_type=F32)
        wcol[i] = acc
        return carry
    lax.fori_loop(0, 8, weigh, 0)

    for s in (1, 2, 3):
        zz = zplace(s)
        arrived(kb.at[zz, c], k_recv.at[zz])
        send(kb.at[zz, c], k_send.at[3 + s], k_sib.at[zz], sib)
    for yy in (y_up, y_dn, y_far):
        arrived(tb.at[yy], t_recv.at[yy])
    for s in range(4):
        zz = zplace(s)
        arrived(kb.at[zz, 1 - c], k_sib.at[zz])

    block = lax.dot_general(
        tb[...].reshape(128, 1024), kb[...].reshape(256, 1024), NT, preferred_element_type=F32
    ).astype(BF16)
    gb[y, :, z, c] = block.reshape(4, 32, 256)

    def part(yy, zz, cc):
        return gb.at[yy, :, zz, cc]

    for s in (1, 2, 3):
        send(part(y, z, c), b_send.at[s], b_recv.at[y, z], at_train(y, zplace(s), c))
    for i, d in enumerate(ring):
        send(part(y, z, c), b_send.at[4 + i], b_recv.at[y, z], d)
    send(part(y, z, c), b_send.at[0], b_sib.at[y, z], sib)
    def most(yy, zz):
        return gb.at[yy, pl.ds(0, 3), zz, c]

    def last(yy, zz):
        return gb.at[yy, 3, zz, c]

    def from_line(s):
        zz = zplace(s)
        arrived(part(y, zz, c), b_recv.at[y, zz])
        for i, d in enumerate(ring):
            send(most(y, zz), b_send.at[4 + 3 * s + i], b_recv.at[y, zz], d)
        send(part(y, zz, c), b_send.at[15 + s], b_sib.at[y, zz], sib)

    from_line(1)
    from_line(2)
    for i, yy in enumerate((y_up, y_dn, y_far)):
        arrived(part(yy, z, c), b_recv.at[yy, z])
        for s in (1, 2, 3):
            send(last(yy, z), l_send.at[3 * i + s - 1], l_recv.at[yy, z], at_train(y, zplace(s), c))
        send(part(yy, z, c), b_send.at[19 + i], b_sib.at[yy, z], sib)
    from_line(3)
    for s in (1, 2, 3):
        zz = zplace(s)
        for i, yy in enumerate((y_up, y_dn, y_far)):
            arrived(most(yy, zz), b_recv.at[yy, zz])
            arrived(last(yy, zz), l_recv.at[yy, zz])
            send(part(yy, zz, c), b_send.at[19 + 3 * s + i], b_sib.at[yy, zz], sib)

    def blocks(h, p):
        side = zh if h == 1 else 1 - zh
        first, second = ((x + 2) % 4, x) if p == 0 else ((x + 1) % 4, (x + 3) % 4)
        return (side * 4 + first) * 128, (side * 4 + second) * 128

    def permute(h, p, yy):
        a, b = blocks(h, p)
        order = order_ref[...]
        j = lax.broadcasted_iota(jnp.int32, (128, 1), 0)
        pick = jnp.concatenate(
            [(order == j + a).astype(F32).astype(BF16), (order == j + b).astype(F32).astype(BF16)], axis=0
        )
        rows = gb[yy].reshape(1024, 256)
        cols = pl.ds(pl.multiple_of(yy * 256, 256), 256)
        ob[2 * h + p, :, cols] = jnp.dot(pick, rows, preferred_element_type=F32).astype(BF16)

    def permute_all(h, p):
        def step(yy, carry):
            permute(h, p, yy)
            return carry
        lax.fori_loop(0, 4, step, 0)

    first_a, first_b = blocks(0, 0)
    j = lax.broadcasted_iota(jnp.int32, (128, 1), 0)

    def permute_from(zz, fresh):
        order = by_place[:, pl.ds(pl.multiple_of(zz * 256, 256), 256)]
        pick = jnp.concatenate(
            [(order == j + first_a).astype(F32).astype(BF16), (order == j + first_b).astype(F32).astype(BF16)], axis=0
        )
        for yy in range(4):
            cols = pl.ds(yy * 256, 256)
            got = jnp.dot(pick, gb[yy, :, zz].reshape(256, 256), preferred_element_type=F32).astype(BF16)
            ob[0, :, cols] = got if fresh else ob[0, :, cols] + got

    loads[5].wait()
    for s in range(4):
        zz = zplace(s)
        for yy in (y, y_up, y_dn, y_far):
            arrived(part(yy, zz, 1 - c), b_sib.at[yy, zz])
        permute_from(zz, s == 0)

    def tile(r, k):
        rows = pl.ds(pl.multiple_of(r * ROWS, ROWS), ROWS)
        t = lax.dot_general(train[rows, :], ob[k], NT, preferred_element_type=F32)
        return t[:, :128] * wcol[r], t[:, 128:] * wcol[r]

    def far_copy(h, i, r, to_right):
        return pltpu.make_async_remote_copy(
            src_ref=s2.at[h, r], dst_ref=(far_l if to_right else far_r).at[h, i], send_sem=s2_send.at[h, r],
            recv_sem=(far_l_recv if to_right else far_r_recv).at[h, i],
            device_id=right if to_right else left, device_id_type=MESH,
        )

    def right_copy(h, r):
        return pltpu.make_async_remote_copy(
            src_ref=sp.at[h, r], dst_ref=got_l.at[h, r], send_sem=sp_send.at[h, r],
            recv_sem=got_l_recv.at[h, r], device_id=right, device_id_type=MESH,
        )

    def left_copy(h, r):
        return pltpu.make_async_remote_copy(
            src_ref=sm.at[h, r], dst_ref=got_r.at[h, r], send_sem=sm_send.at[h, r],
            recv_sem=got_r_recv.at[h, r], device_id=left, device_id_type=MESH,
        )

    def z_copy(r):
        return pltpu.make_async_remote_copy(
            src_ref=zs.at[r], dst_ref=zr.at[r], send_sem=z_send.at[r],
            recv_sem=z_recv.at[r], device_id=across, device_id_type=MESH,
        )

    def out_copy(r):
        rows = pl.ds(pl.multiple_of(r * ROWS, ROWS), ROWS)
        return pltpu.make_async_copy(own.at[1, r], out_ref.at[rows, :], out_sem.at[r])

    def early_copy(half):
        return pltpu.make_async_remote_copy(
            src_ref=s2.at[0, 3 + 4 * half], dst_ref=zf.at[half], send_sem=s2_send.at[0, 3 + 4 * half],
            recv_sem=zf_recv.at[half], device_id=across, device_id_type=MESH,
        )

    def far_blocks(h, first, last):
        def step(i, carry):
            for half in (0, 1):
                r = i + 4 * half
                a, b = tile(r, 2 * h)
                s2[h, r] = a.astype(BF16)
                own[h, r] = b
                far_copy(h, i, r, half == 0).start()
            return carry
        lax.fori_loop(first, last, step, 0)

    def far_last(h):
        for half in (0, 1):
            r = 3 + 4 * half
            a, b = tile(r, 2 * h)
            own[h, r] = b
            if h == 0:
                s2[h, r] = a.astype(BF16)
                early_copy(half).start()
            else:
                early_copy(half).wait_recv()
                s2[h, r] = (a + zf[half].astype(F32)).astype(BF16)
                far_copy(h, 3, r, half == 0).start()

    def near_block(h, i, add):
        p, m = tile(i, 2 * h + 1)
        sm[h, i] = m.astype(BF16)
        left_copy(h, i).start()
        if add:
            far_copy(h, i, i, True).wait_recv()
            p += far_l[h, i].astype(F32)
        sp[h, i] = p.astype(BF16)
        right_copy(h, i).start()
        r = i + 4
        p, m = tile(r, 2 * h + 1)
        sp[h, r] = p.astype(BF16)
        right_copy(h, r).start()
        if add:
            far_copy(h, i, r, False).wait_recv()
            m += far_r[h, i].astype(F32)
        sm[h, r] = m.astype(BF16)
        left_copy(h, r).start()

    def near_blocks(h, first, last):
        def step(i, carry):
            near_block(h, i, True)
            return carry
        lax.fori_loop(first, last, step, 0)

    def add_up(h, first, last):
        def step(i, carry):
            for half in (0, 1):
                r = i + 4 * half
                right_copy(h, r).wait_recv()
                left_copy(h, r).wait_recv()
                v = own[h, r] + got_l[h, r].astype(F32) + got_r[h, r].astype(F32)
                if h == 0:
                    zs[r] = v.astype(BF16)
                    z_copy(r).start()
                else:
                    z_copy(r).wait_recv()
                    own[1, r] = (v + zr[r].astype(F32)) * 0.125
                    out_copy(r).start()
            return carry
        lax.fori_loop(first, last, step, 0)

    @pl.when(zh == 0)
    def _():
        pl.semaphore_wait(ready, 1)

    far_blocks(0, 0, 1)
    far_last(0)
    far_blocks(0, 1, 2)
    permute_all(0, 1)
    near_block(0, 3, False)
    far_blocks(0, 2, 3)
    near_blocks(0, 0, 2)
    permute_all(1, 0)
    add_up(0, 3, 4)
    near_blocks(0, 2, 3)
    far_blocks(1, 0, 3)
    add_up(0, 0, 1)
    permute_all(1, 1)
    add_up(0, 1, 2)
    far_last(1)
    add_up(0, 2, 3)
    near_blocks(1, 0, 4)
    add_up(1, 0, 4)

    for cp in started:
        cp.wait_send()

    def drain(r, carry):
        for h in (0, 1):
            far_copy(h, 0, r, True).wait_send()
            right_copy(h, r).wait_send()
            left_copy(h, r).wait_send()
        z_copy(r).wait_send()
        out_copy(r).wait()
        return carry
    lax.fori_loop(0, 8, drain, 0)


def shards(train_feat, test_feat, kernel_inv, bucket_weight, bucket, test_order):
    anywhere = pl.BlockSpec(memory_space=pl.ANY)
    vmem = pl.BlockSpec(memory_space=pltpu.VMEM)
    dma = pltpu.SemaphoreType.DMA
    return pl.pallas_call(
        kernel,
        out_shape=jax.ShapeDtypeStruct((2048, 128), F32),
        in_specs=[anywhere] * 6,
        out_specs=pl.BlockSpec(memory_space=pl.ANY),
        scratch_shapes=[
            pltpu.VMEM((1, 16), F32),
            pltpu.VMEM((1, 2048), jnp.int32),
            pltpu.VMEM((1, 1024), jnp.int32),
            pltpu.VMEM((1, 1024), jnp.int32),
            pltpu.VMEM((2048, 1024), BF16),
            pltpu.VMEM((4, 32, 1024), BF16),
            pltpu.VMEM((4, 2, 32, 1024), BF16),
            pltpu.VMEM((4, 4, 4, 2, 32, 256), BF16),
            pltpu.VMEM((4, 256, 1024), BF16),
            pltpu.VMEM((8, ROWS, 128), F32),
            pltpu.VMEM((2, 8, ROWS, 128), BF16),
            pltpu.VMEM((2, 8, ROWS, 128), BF16),
            pltpu.VMEM((2, 8, ROWS, 128), BF16),
            pltpu.VMEM((2, 4, ROWS, 128), BF16),
            pltpu.VMEM((2, 4, ROWS, 128), BF16),
            pltpu.VMEM((2, 8, ROWS, 128), BF16),
            pltpu.VMEM((2, 8, ROWS, 128), BF16),
            pltpu.VMEM((2, 8, ROWS, 128), F32),
            pltpu.VMEM((8, ROWS, 128), BF16),
            pltpu.VMEM((8, ROWS, 128), BF16),
            pltpu.VMEM((2, ROWS, 128), BF16),
            pltpu.SemaphoreType.REGULAR,
            dma((8,)),
            dma((6,)),
            dma((3,)),
            dma((4,)),
            dma((7,)),
            dma((4,)),
            dma((4,)),
            dma((31,)),
            dma((4, 4)),
            dma((4, 4)),
            dma((9,)),
            dma((4, 4)),
            dma((2, 8)),
            dma((2, 8)),
            dma((2, 8)),
            dma((2, 4)),
            dma((2, 4)),
            dma((2, 8)),
            dma((2, 8)),
            dma((8,)),
            dma((8,)),
            dma((2,)),
        ],
        compiler_params=pltpu.CompilerParams(
            collective_id=0, has_side_effects=True, vmem_limit_bytes=60 * 1024 * 1024
        ),
        name="scores",
    )(
        train_feat[0], test_feat[0], kernel_inv[0], bucket_weight,
        bucket.reshape(1, 2048), test_order.reshape(1, 1024),
    )


def solution(mesh):
    return jax.shard_map(
        shards, mesh=mesh,
        in_specs=(P("ckpt", "train", None), P("ckpt", "train", None), P("ckpt", "train", None),
                  P("ckpt", None), P("train"), P(None)),
        out_specs=P("train", "ckpt"), check_vma=False,
    )
```
